32 devices in a mesh: member: 2 (over x), fsdp: 16 (over z, y, core).
Axes of the slice: x: 2, y: 2, z: 4, core: 2. Of those that a mesh axis runs over, the one named last changes fastest.
Arguments:
- context: bfloat16 [4, 2048, 2048], P(None, 'fsdp', 'member'), may hold values from -6 to 6
- residual: bfloat16 [2048, 2048], P('fsdp', 'member'), may hold values from -6 to 6
- out_weight: bfloat16 [2048, 2048], P('fsdp', 'member'), may hold values from -0.1875 to 0.1875
- in_factor: bfloat16 [4, 2048], P(None, 'member'), may hold values from 0.25 to 1.75
- out_factor: bfloat16 [4, 2048], P(None, 'member'), may hold values from 0.25 to 1.75
- cotangent: bfloat16 [4, 2048, 2048], P(None, 'fsdp', 'member'), may hold values from -0.796875 to 0.796875
Outputs:
- hidden: bfloat16 [4, 2048, 2048], P(None, 'fsdp', 'member')
- grad_context: bfloat16 [4, 2048, 2048], P(None, 'fsdp', 'member')
- grad_weight: float32 [2048, 2048], P('fsdp', 'member')
- grad_in_factor: float32 [4, 2048], P(None, 'member')
- grad_out_factor: float32 [4, 2048], P(None, 'member')
- grad_residual: float32 [2048, 2048], P('fsdp', 'member')
The draws below stay inside these ranges and needn't reach their ends.
All inputs are finite; a program needn't handle non-finite values.
Results may differ from the reference program's by a relative error of at most 0.013.
Values may be sent and summed in bfloat16 or wider, within the bound.
A program may use at most 64 MiB of HBM per device.

```python
import jax
import jax.numpy as jnp
from jax import lax

INNER = 2048
DW = 2048
ENSEMBLE = 4
TOKENS = 2048
N_MEMBER = 2


def raised(array, own_key, source, target, blocks, factor):
    owner, partner = [(jnp.arange(array.shape[dim]) // (array.shape[dim] // blocks)).reshape([-1 if axis == dim else 1 for axis in range(array.ndim)]) for dim in (source, target)]
    chosen = jax.random.permutation(own_key, blocks)[partner]
    strong = (owner == chosen) | (owner == (partner + blocks // 2) % blocks)
    return jnp.where(strong, factor * array, array)


def shard_levels(rng, shape, pieces, least, high):
    factor_of, own = 1.0, jax.random.fold_in(rng, 6)
    for dim, parts in pieces:
        heights = jnp.exp(jax.random.uniform(jax.random.fold_in(own, dim), (parts,), jnp.float32, least / len(pieces), high / len(pieces)))
        factor_of = factor_of * jnp.repeat(heights, shape[dim] // parts).reshape([-1 if axis == dim else 1 for axis in range(len(shape))])
    return factor_of


def gaussian(rng, extent, scale, most, split=(), held_as=jnp.bfloat16):
    result = jax.random.normal(rng, extent, jnp.float32) * scale
    if len(split) > 0:
        result = shard_levels(rng, extent, split, -0.22, 0.18) * result
    return jnp.clip(result, min=-most, max=most).astype(held_as)


def gaussian_with(stream_key, dims, deviation, limit, shards, heavy, dtype=jnp.bfloat16):
    result = deviation * jax.random.normal(stream_key, dims, jnp.float32)
    if shards:
        result = result * shard_levels(stream_key, dims, shards, -0.22, 0.18)
    return jnp.clip(raised(result, jax.random.fold_in(stream_key, 3), *heavy), -limit, limit).astype(dtype)


def setup_inputs(seed: int = 0) -> dict:
    keys = jax.random.split(jax.random.key(seed), 7)
    return {
        "context": gaussian_with(keys[0], (ENSEMBLE, TOKENS, INNER), 1.0, 6.0, ((1, 16), (2, 2)), (1, 2, 16, 2.0)),
        "residual": gaussian(keys[1], (TOKENS, DW), 1.0, 6.0, ((0, 16), (1, 2))),
        "out_weight": gaussian_with(keys[2], (INNER, DW), INNER ** -0.5, 0.1875, ((0, 16), (1, 2)), (1, 0, 16, 2.0)),
        "in_factor": jnp.clip(1.0 + 0.15 * jax.random.normal(keys[3], (ENSEMBLE, INNER), jnp.float32), 0.25, 1.75).astype(jnp.bfloat16),
        "out_factor": jnp.clip(1.0 + 0.15 * jax.random.normal(keys[4], (ENSEMBLE, DW), jnp.float32), 0.25, 1.75).astype(jnp.bfloat16),
        "cotangent": gaussian(keys[5], (ENSEMBLE, TOKENS, DW), 0.1, 0.796875, ((1, 16), (2, 2))),
    }


def reference(context, residual, out_weight, in_factor, out_factor, cotangent):
    resid_wide = residual.astype(jnp.float32)
    block_width = DW // N_MEMBER

    def member_step(running, member_items):
        weight_sum, resid_sum = running
        context_rows, in_scale, out_scale, grad_rows = member_items
        in_wide = in_scale.astype(jnp.float32)
        out_wide = out_scale.astype(jnp.float32)
        scaled_context = (context_rows.astype(jnp.float32) * in_wide).astype(jnp.bfloat16)
        scaled_grad = (grad_rows.astype(jnp.float32) * out_wide).astype(jnp.bfloat16)
        projected = jnp.dot(scaled_context, out_weight, preferred_element_type=jnp.float32)
        hidden = (resid_wide + projected * out_wide).astype(jnp.bfloat16)
        backward = jnp.zeros((TOKENS, INNER), jnp.float32)
        for block_index in range(N_MEMBER):
            lower = block_index * block_width
            upper = lower + block_width
            partial_value = jnp.dot(scaled_grad[:, lower:upper], out_weight[:, lower:upper].T, preferred_element_type=jnp.float32).astype(jnp.bfloat16)
            backward = backward + partial_value.astype(jnp.float32)
        grad_context = (backward * in_wide).astype(jnp.bfloat16)
        grad_in = jnp.sum(context_rows.astype(jnp.float32) * backward, axis=0)
        grad_out = jnp.sum(grad_rows.astype(jnp.float32) * projected, axis=0)
        weight_sum = weight_sum + jnp.dot(scaled_context.T, scaled_grad, preferred_element_type=jnp.float32)
        resid_sum = resid_sum + grad_rows.astype(jnp.float32)
        return (weight_sum, resid_sum), (hidden, grad_context, grad_in, grad_out)

    start_state = (jnp.zeros((INNER, DW), jnp.float32), jnp.zeros((TOKENS, DW), jnp.float32))
    final_state, outputs = lax.scan(member_step, start_state, (context, in_factor, out_factor, cotangent))
    grad_weight, grad_residual = final_state
    hidden, grad_context, grad_in_factor, grad_out_factor = outputs
    return hidden, grad_context, grad_weight, grad_in_factor, grad_out_factor, grad_residual
```

```python
import functools

import jax
import jax.numpy as jnp
from jax import lax
from jax.experimental import pallas as pl
from jax.experimental.pallas import tpu as pltpu
from jax.sharding import PartitionSpec as P

F32 = jnp.float32
BF16 = jnp.bfloat16


def general(context, residual, out_weight, in_factor, out_factor, cotangent):
    in_wide = in_factor.astype(jnp.float32)
    out_wide = out_factor.astype(jnp.float32)
    scaled_local = (context.astype(jnp.float32) * in_wide[:, None, :]).astype(jnp.bfloat16)
    scaled_grad = (cotangent.astype(jnp.float32) * out_wide[:, None, :]).astype(jnp.bfloat16)
    scaled_context = lax.all_gather(scaled_local, "member", axis=2, tiled=True)
    weight = lax.all_gather(out_weight, "fsdp", axis=0, tiled=True)
    projected = jnp.einsum(
        "eti,id->etd", scaled_context, weight, preferred_element_type=jnp.float32
    )
    partial_value = jnp.einsum(
        "etd,id->eti", scaled_grad, weight, preferred_element_type=jnp.float32
    )
    hidden = (residual.astype(jnp.float32)[None] + projected * out_wide[:, None, :]).astype(
        jnp.bfloat16
    )
    backward = lax.psum_scatter(
        partial_value.astype(jnp.bfloat16), "member", scatter_dimension=2, tiled=True
    ).astype(jnp.float32)
    grad_context = (backward * in_wide[:, None, :]).astype(jnp.bfloat16)
    grad_in_local = jnp.sum(context.astype(jnp.float32) * backward, axis=1)
    grad_out_local = jnp.sum(cotangent.astype(jnp.float32) * projected, axis=1)
    grad_in, grad_out = lax.psum((grad_in_local, grad_out_local), "fsdp")
    grad_block = jnp.einsum(
        "eti,etd->id", scaled_context, scaled_grad, preferred_element_type=jnp.float32
    )
    grad_weight = lax.psum_scatter(grad_block, "fsdp", scatter_dimension=0, tiled=True)
    grad_residual = jnp.sum(cotangent.astype(jnp.float32), axis=0)
    return (hidden, grad_context, grad_weight, grad_in, grad_out, grad_residual)


def kernel(
    C,
    ctx_h, res_h, w_h, inf_h, outf_h, cot_h,
    hid, gc, gw, gi, go, gr,
    ctx, cot, res, inf, outf, cbuf, infx, sc, sg, wb, proj, part, xrecv, gall, psend, precv, rsend, rrecv, arb, arr, swp,
    ld_sem, cx_ss, cx_rs, ag_ss, ag_rs, pt_ss, pt_rs, px_ss, px_rs, ps_ss, ps_rs, rs_ss, rs_rs, ar_ss, ar_rs,
):
    E, T, H = ctx.shape
    R = w_h.shape[0]
    R2 = 2 * R
    S = R // 2
    half = C // 2
    far = C // 2
    bits = []
    b = 1
    while b < 2 * C:
        bits.append(b)
        b *= 2

    m = lax.axis_index("member")
    f = lax.axis_index("fsdp")
    c = f % 2
    q = f // 2
    p = (1 - q % 2) * (q // 2) + (q % 2) * (C - 1 - q // 2)

    def chip_at(offset):
        pos = (p + offset + C) % C
        y = pos // half
        return 2 * ((1 - y) * pos + y * (C - 1 - pos)) + y

    peer = (1 - m, f)
    partner = (m, q * 2 + 1 - c)
    nxt = (m, chip_at(1) * 2 + c)
    prv = (m, chip_at(-1) * 2 + c)
    side = (nxt, prv)
    sign = (1, -1)
    flips = [(m, f + bit * (1 - 2 * ((f // bit) % 2))) for bit in bits]

    def rc(src, dst, ss, rs, dev):
        return pltpu.make_async_remote_copy(
            src_ref=src, dst_ref=dst, send_sem=ss, recv_sem=rs,
            device_id=dev, device_id_type=pl.DeviceIdType.MESH,
        )

    barrier = pltpu.get_barrier_semaphore()
    greet = [peer, partner, nxt, prv]
    for dev in greet:
        pl.semaphore_signal(barrier, inc=1, device_id=dev, device_id_type=pl.DeviceIdType.MESH)

    def rows_of(core):
        return pl.ds(pl.multiple_of(core * R, R), R)

    def load(i, src, dst):
        copy = pltpu.make_async_copy(src, dst, ld_sem.at[i])
        copy.start()
        return copy

    ld_inf = load(0, inf_h, inf)
    ld_ctx = load(1, ctx_h, ctx)
    ld_outf = load(2, outf_h, outf)
    ld_cot = load(3, cot_h, cot)
    ld_w = load(4, w_h, wb.at[q, rows_of(c)])
    ld_res = load(5, res_h, res)

    order = [chip_at(-far)] + [chip_at(s * (far - k)) for k in range(1, far) for s in sign] + [q]

    def ranked(side_of):
        found = [0] * half
        count = 0
        for chip in order:
            member = chip // half == side_of
            for n in range(half):
                found[n] = jnp.where(jnp.logical_and(member, count == n), chip, found[n])
            count = count + jnp.where(member, 1, 0)
        return found

    mine = ranked(m)
    theirs = ranked(1 - m)

    def cols_of(chip):
        return pl.ds(pl.multiple_of((chip % half) * R2, R2), R2)

    def cx(n):
        return rc(ctx_h.at[:, :, cols_of(mine[n])], cbuf.at[n], cx_ss.at[n], cx_rs.at[n], peer)

    cxf = rc(inf_h, infx, cx_ss.at[half], cx_rs.at[half], peer)

    def sub(core, u):
        return pl.ds(pl.multiple_of(core * R + u * S, S), S)

    def subs(d, s):
        return (0, 1) if s < far else (d,)

    def ag(d, s, u, shift):
        qq = chip_at(-sign[d] * (s - 1 + shift))
        dst = wb.at[qq, sub(c, u)]
        src = w_h.at[pl.ds(u * S, S)] if (s == 1 and shift == 0) else dst
        return rc(src, dst, ag_ss.at[d, s - 1, u], ag_rs.at[d, s - 1, u], side[d])

    def pt(k, u, offset, own):
        qq = chip_at(offset)
        dst = wb.at[qq, sub(c if own else 1 - c, u)]
        src = w_h.at[pl.ds(u * S, S)] if (own and k == 0) else dst
        return rc(src, dst, pt_ss.at[k, u], pt_rs.at[k, u], partner)

    sends = []

    def go_send(copy):
        copy.start()
        sends.append(copy)

    pl.semaphore_wait(barrier, len(greet))
    go_send(cxf)
    for n in range(half):
        go_send(cx(n))
    for u in range(2):
        for d in range(2):
            go_send(ag(d, 1, u, 0))
        go_send(pt(0, u, 0, True))

    ld_inf.wait()
    ld_ctx.wait()
    inw = inf[...].astype(F32)
    for e in range(E):
        v = (ctx[e].astype(F32) * inw[e:e + 1]).astype(BF16)
        for j in range(half):
            sc[m * half + j, e * T:(e + 1) * T, :] = v[:, j * R2:(j + 1) * R2]
    ld_outf.wait()
    ld_cot.wait()
    outw = outf[...].astype(F32)
    for e in range(E):
        sg[e * T:(e + 1) * T, :] = (cot[e].astype(F32) * outw[e:e + 1]).astype(BF16)

    def px(qq):
        return rc(part.at[qq], xrecv.at[qq % half], px_ss.at[qq % half], px_rs.at[qq % half], peer)

    def ps(qq):
        return rc(psend.at[qq], precv.at[qq], ps_ss.at[qq], ps_rs.at[qq], partner)

    def gw_one(qq):
        g = lax.dot_general(sc[qq], sg[...], (((0,), (0,)), ((), ())), preferred_element_type=F32)
        gall[qq, 0] = g[:R]
        gall[qq, 1] = g[R:]
        psend[qq] = gall[qq, 1 - c].astype(BF16)
        ps(qq).start()

    def order_at(i):
        return chip_at((far - (i + 1) // 2) * (1 - 2 * ((i + 1) % 2)))

    def gw_mine():
        def body(i, carry):
            qq = order_at(i)

            @pl.when(qq // half == m)
            def _():
                gw_one(qq)
            return carry
        lax.fori_loop(0, C, body, 0)

    def project(qq):
        proj[...] += jnp.dot(sc[qq], wb[qq], preferred_element_type=F32)

    def process(offsets):
        def body(j, carry):
            off = offsets[0] if len(offsets) == 1 else offsets[0] + j * (offsets[1] - offsets[0])
            qq = chip_at(off)
            part[qq] = lax.dot_general(
                sg[...], wb[qq], (((1,), (1,)), ((), ())), preferred_element_type=F32
            ).astype(BF16)

            @pl.when(qq // half != m)
            def _():
                px(qq).start()

            @pl.when(qq // half == m)
            def _():
                project(qq)
            return carry
        lax.fori_loop(0, len(offsets), body, 0)

    def rs(d, k, u):
        rows = pl.ds(u * S, S)
        return rc(rsend.at[d, k, rows], rrecv.at[d, k, rows], rs_ss.at[d, k, u], rs_rs.at[d, k, u], side[d])

    def chip_sum(qq, u):
        rows = slice(u * S, (u + 1) * S)
        return gall[qq, c, rows, :] + precv[qq, rows, :].astype(F32)

    def rs_sub(k, late):
        if k == 0:
            ps(chip_at(-far)).wait_recv()
        for d in range(2):
            qq = chip_at(sign[d] * (far - k)) if k else chip_at(-far)
            if k and not late:
                ps(qq).wait_recv()
            u = d if late else 1 - d
            rows = slice(u * S, (u + 1) * S)
            v = chip_sum(qq, u)
            if k > 1 or (k == 1 and late):
                rs(d, k - 1, u).wait_recv()
                v = v + rrecv[d, k - 1, rows, :].astype(F32)
            rsend[d, k, rows, :] = v.astype(BF16)
            go_send(rs(d, k, u))

    proj[...] = jnp.zeros(proj.shape, F32)
    gw_mine()
    ld_w.wait()
    for u in range(2):
        pt(0, u, 0, False).wait_recv()
    process([0])

    def scale_in(n):
        cx(n).wait_recv()
        for e in range(E):
            wide = infx[e:e + 1, cols_of(theirs[n])].astype(F32)
            sc[theirs[n], e * T:(e + 1) * T, :] = (cbuf[n, e].astype(F32) * wide).astype(BF16)
        gw_one(theirs[n])

    for s in range(1, far):
        for u in range(2):
            for d in range(2):
                ag(d, s, u, 1).wait_recv()
                if u in subs(d, s + 1):
                    go_send(ag(d, s + 1, u, 0))
                go_send(pt(d * (far - 1) + s, u, -sign[d] * s, True))
        if s == far - 1:
            rs_sub(0, True)
        if s == 1:
            gr[...] = jnp.sum(cot[...].astype(F32), axis=0)
        for u in range(2):
            for d in range(2):
                pt(d * (far - 1) + s, u, -sign[d] * s, False).wait_recv()
        process([-s, s])
        if s == 1:
            cxf.wait_recv()
        if s < half:
            scale_in(s - 1)
    for n in range(1, far - 1):
        project(theirs[n])
    rs_sub(1, False)
    for d in range(2):
        ag(d, far, d, 1).wait_recv()
        go_send(pt(2 * far - 1, d, far, True))
    for d in range(2):
        pt(2 * far - 1, d, far, False).wait_recv()
    process([far])
    project(theirs[0])
    for n in range(far - 1, half):
        scale_in(n)
        project(theirs[n])

    ld_res.wait()
    resw = res[...].astype(F32)
    for e in range(E):
        pe = proj[e * T:(e + 1) * T, :]
        hid[e] = (resw + pe * outw[e:e + 1]).astype(BF16)
        arb[0, 2 * E + e:2 * E + e + 1, :] = jnp.sum(cot[e].astype(F32) * pe, axis=0, keepdims=True)
    for n in range(half):
        for e in range(E):
            rows = slice(e * T, (e + 1) * T)
            cols = slice(n * R2, (n + 1) * R2)
            a = ctx[e, :, cols].astype(F32) * part[m * half + n, rows, :].astype(F32)
            arb[0, e:e + 1, cols] = jnp.sum(a, axis=0, keepdims=True)
            a = cbuf[n, e].astype(F32) * part[theirs[n], rows, :].astype(F32)
            arb[0, E + e:E + e + 1, cols_of(theirs[n])] = jnp.sum(a, axis=0, keepdims=True)

    def ar(i):
        return rc(arb.at[i], arr.at[i], ar_ss.at[i], ar_rs.at[i], flips[i])

    swap = rc(swp.at[0], swp.at[1], cx_ss.at[half + 1], cx_rs.at[half + 1], peer)

    def ar_step(i):
        ar(i).wait_recv()
        total = arb[i] + arr[i]
        if i + 1 < len(bits):
            arb[i + 1] = total
            go_send(ar(i + 1))
        else:
            swp[0] = total[E:2 * E]
            go_send(swap)
            gi[...] = total[:E]
            go[...] = total[2 * E:]

    def finish(n):
        chip = mine[n]
        slot = chip % half
        rc(xrecv.at[slot], xrecv.at[slot], px_ss.at[slot], px_rs.at[slot], peer).wait_recv()
        for e in range(E):
            rows = slice(e * T, (e + 1) * T)
            be = part[chip, rows, :].astype(F32) + xrecv[slot, rows, :].astype(F32)
            wide = inf[e:e + 1, cols_of(chip)].astype(F32)
            gc[e, :, cols_of(chip)] = (be * wide).astype(BF16)

    go_send(ar(0))
    rs_sub(1, True)
    ar_step(0)
    done = 1
    pending = half
    for k in range(2, far):
        for late in (False, True):
            rs_sub(k, late)
            if late and done < len(bits):
                ar_step(done)
                done += 1
        if pending > 2:
            pending -= 1
            finish(pending)
    ps(q).wait_recv()

    def own(u):
        rows = slice(u * S, (u + 1) * S)
        total = chip_sum(q, u)
        for d in range(2):
            rs(d, far - 1, u).wait_recv()
            total = total + rrecv[d, far - 1, rows, :].astype(F32)
        gw[rows, :] = total

    while done < len(bits):
        ar_step(done)
        done += 1
    own(0)
    own(1)
    while pending > 0:
        pending -= 1
        finish(pending)
    swap.wait_recv()
    gi[...] += swp[1]

    for copy in sends:
        copy.wait_send()

    def drain(j, carry):
        ps(j).wait_send()
        return carry
    lax.fori_loop(0, C, drain, 0)
    for n in range(half):
        slot = theirs[n] % half
        rc(part.at[theirs[n]], xrecv.at[slot], px_ss.at[slot], px_rs.at[slot], peer).wait_send()


def fused(C, context, residual, out_weight, in_factor, out_factor, cotangent):
    E, T, H = context.shape
    M = E * T
    R = out_weight.shape[0]
    half = C // 2
    far = half
    steps = (2 * C).bit_length() - 1
    vm = pl.BlockSpec(memory_space=pltpu.VMEM)
    hbm = pl.BlockSpec(memory_space=pl.ANY)
    dma = pltpu.SemaphoreType.DMA
    shape = jax.ShapeDtypeStruct
    results = pl.pallas_call(
        functools.partial(kernel, C),
        out_shape=(
            pltpu.VMEM((E, T, H), BF16),
            pltpu.VMEM((E, T, H), BF16),
            pltpu.VMEM((R, H), F32),
            pltpu.VMEM((E, H), F32),
            pltpu.VMEM((E, H), F32),
            pltpu.VMEM((T, H), F32),
        ),
        in_specs=[hbm] * 6,
        out_specs=tuple([vm] * 6),
        scratch_shapes=[
            pltpu.VMEM((E, T, H), BF16),
            pltpu.VMEM((E, T, H), BF16),
            pltpu.VMEM((T, H), BF16),
            pltpu.VMEM((E, H), BF16),
            pltpu.VMEM((E, H), BF16),
            pltpu.VMEM((half, E, T, 2 * R), BF16),
            pltpu.VMEM((E, H), BF16),
            pltpu.VMEM((C, M, 2 * R), BF16),
            pltpu.VMEM((M, H), BF16),
            pltpu.VMEM((C, 2 * R, H), BF16),
            pltpu.VMEM((M, H), F32),
            pltpu.VMEM((C, M, 2 * R), BF16),
            pltpu.VMEM((half, M, 2 * R), BF16),
            pltpu.VMEM((C, 2, R, H), F32),
            pltpu.VMEM((C, R, H), BF16),
            pltpu.VMEM((C, R, H), BF16),
            pltpu.VMEM((2, far, R, H), BF16),
            pltpu.VMEM((2, far, R, H), BF16),
            pltpu.VMEM((steps, 3 * E, H), F32),
            pltpu.VMEM((steps, 3 * E, H), F32),
            pltpu.VMEM((2, E, H), F32),
            dma((6,)),
            dma((half + 2,)),
            dma((half + 2,)),
            dma((2, far, 2)),
            dma((2, far, 2)),
            dma((2 * far, 2)),
            dma((2 * far, 2)),
            dma((half,)),
            dma((half,)),
            dma((C,)),
            dma((C,)),
            dma((2, far, 2)),
            dma((2, far, 2)),
            dma((steps,)),
            dma((steps,)),
        ],
        compiler_params=pltpu.CompilerParams(
            collective_id=0, has_side_effects=True, vmem_limit_bytes=62208 * 1024
        ),
    )(context, residual, out_weight, in_factor, out_factor, cotangent)
    return pl.pallas_call(
        deliver,
        out_shape=tuple(shape(r.shape, r.dtype) for r in results),
        in_specs=[hbm] * 6,
        out_specs=tuple([hbm] * 6),
        scratch_shapes=[dma((6,))],
        compiler_params=pltpu.CompilerParams(vmem_limit_bytes=1024 * 1024),
    )(*results)


def deliver(*refs):
    copies = [pltpu.make_async_copy(refs[i], refs[6 + i], refs[12].at[i]) for i in range(6)]
    for copy in copies:
        copy.start()
    for copy in copies:
        copy.wait()


def solution(mesh):
    in_specs = (
        P(None, "fsdp", "member"),
        P("fsdp", "member"),
        P("fsdp", "member"),
        P(None, "member"),
        P(None, "member"),
        P(None, "fsdp", "member"),
    )
    out_specs = (
        P(None, "fsdp", "member"),
        P(None, "fsdp", "member"),
        P("fsdp", "member"),
        P(None, "member"),
        P(None, "member"),
        P("fsdp", "member"),
    )
    members = mesh.shape["member"]
    chips = mesh.shape["fsdp"] // 2
    if members == 2 and chips >= 8 and chips & (chips - 1) == 0:
        per_device = functools.partial(fused, chips)
    else:
        per_device = general
    return jax.shard_map(
        per_device, mesh=mesh, in_specs=in_specs, out_specs=out_specs, check_vma=False
    )
```

```python
import functools

import jax
import jax.numpy as jnp
from jax import lax
from jax.experimental import pallas as pl
from jax.experimental.pallas import tpu as pltpu
from jax.sharding import PartitionSpec as P

F32 = jnp.float32
BF16 = jnp.bfloat16


def general(context, residual, out_weight, in_factor, out_factor, cotangent):
    in_wide = in_factor.astype(jnp.float32)
    out_wide = out_factor.astype(jnp.float32)
    scaled_local = (context.astype(jnp.float32) * in_wide[:, None, :]).astype(jnp.bfloat16)
    scaled_grad = (cotangent.astype(jnp.float32) * out_wide[:, None, :]).astype(jnp.bfloat16)
    scaled_context = lax.all_gather(scaled_local, "member", axis=2, tiled=True)
    weight = lax.all_gather(out_weight, "fsdp", axis=0, tiled=True)
    projected = jnp.einsum(
        "eti,id->etd", scaled_context, weight, preferred_element_type=jnp.float32
    )
    partial_value = jnp.einsum(
        "etd,id->eti", scaled_grad, weight, preferred_element_type=jnp.float32
    )
    hidden = (residual.astype(jnp.float32)[None] + projected * out_wide[:, None, :]).astype(
        jnp.bfloat16
    )
    backward = lax.psum_scatter(
        partial_value.astype(jnp.bfloat16), "member", scatter_dimension=2, tiled=True
    ).astype(jnp.float32)
    grad_context = (backward * in_wide[:, None, :]).astype(jnp.bfloat16)
    grad_in_local = jnp.sum(context.astype(jnp.float32) * backward, axis=1)
    grad_out_local = jnp.sum(cotangent.astype(jnp.float32) * projected, axis=1)
    grad_in, grad_out = lax.psum((grad_in_local, grad_out_local), "fsdp")
    grad_block = jnp.einsum(
        "eti,etd->id", scaled_context, scaled_grad, preferred_element_type=jnp.float32
    )
    grad_weight = lax.psum_scatter(grad_block, "fsdp", scatter_dimension=0, tiled=True)
    grad_residual = jnp.sum(cotangent.astype(jnp.float32), axis=0)
    return (hidden, grad_context, grad_weight, grad_in, grad_out, grad_residual)


def kernel(
    C,
    ctx_h, res_h, w_h, inf_h, outf_h, cot_h,
    hid_o, gc_o, gw_o, gi_o, go_o, gr_o,
    hid, gc, gw, gi, go, gr,
    ctx, cot, res, inf, outf, cbuf, infx, sc, sg, wb, proj, part, xrecv, gall, psend, precv, rsend, rrecv,
    arb, ars, arr, fin, swp, swr,
    ld_sem, st_sem, out_sem, cx_rs, ag_rs, pt_rs, px_rs, ps_rs, rs_rs, ar_rs,
):
    E, T, H = ctx.shape
    R = w_h.shape[0]
    R2 = 2 * R
    S = R // 2
    half = C // 2
    far = C // 2
    lines = C // 2
    H2 = H // 2
    pieces = 2 * far - 1

    m = lax.axis_index("member")
    f = lax.axis_index("fsdp")
    c = f % 2
    q = f // 2
    p = (1 - q % 2) * (q // 2) + (q % 2) * (C - 1 - q // 2)

    def chip_at(offset):
        pos = (p + offset + C) % C
        y = pos // half
        return 2 * ((1 - y) * pos + y * (C - 1 - pos)) + y

    peer = (1 - m, f)
    partner = (m, q * 2 + 1 - c)
    nxt = (m, chip_at(1) * 2 + c)
    prv = (m, chip_at(-1) * 2 + c)
    side = (nxt, prv)
    sign = (1, -1)
    cross = (1 - m, q * 2 + 1 - c)
    beside = (m, f + 2 - 4 * (q % 2))

    def along(i):
        line = q // 2
        other = 0
        bit = 1
        while bit < lines:
            own = (line // bit) % 2
            other = other + bit * (1 - own if i & bit else own)
            bit *= 2
        return (m, f + 4 * (other - line))


    def rc(src, dst, ss, rs, dev):
        return pltpu.make_async_remote_copy(
            src_ref=src, dst_ref=dst, send_sem=ss, recv_sem=rs,
            device_id=dev, device_id_type=pl.DeviceIdType.MESH,
        )

    barrier = pltpu.get_barrier_semaphore()
    greet = [peer, partner, nxt, prv]
    for dev in greet:
        pl.semaphore_signal(barrier, inc=1, device_id=dev, device_id_type=pl.DeviceIdType.MESH)

    def rows_of(core):
        return pl.ds(pl.multiple_of(core * R, R), R)

    def load(i, src, dst):
        copy = pltpu.make_async_copy(src, dst, ld_sem.at[i])
        copy.start()
        return copy

    def store(i, src, dst):
        pltpu.make_async_copy(src, dst, st_sem.at[i]).start()

    CX, CXF, AG, PT, PX, PS, RS, AR, SWAP, FIN = range(10)

    ld_inf = load(0, inf_h, inf)
    ld_ctx = load(1, ctx_h, ctx)
    ld_outf = load(2, outf_h, outf)
    ld_cot = load(3, cot_h, cot)
    ld_w = load(4, w_h, wb.at[q, rows_of(c)])
    ld_res = load(5, res_h, res)

    order = [chip_at(-far)] + [chip_at(s * (far - k)) for k in range(1, far) for s in sign] + [q]

    def ranked(side_of):
        found = [0] * half
        count = 0
        for chip in order:
            member = chip // half == side_of
            for n in range(half):
                found[n] = jnp.where(jnp.logical_and(member, count == n), chip, found[n])
            count = count + jnp.where(member, 1, 0)
        return found

    mine = ranked(m)
    theirs = ranked(1 - m)

    def cols_of(chip):
        return pl.ds(pl.multiple_of((chip % half) * R2, R2), R2)

    def cx(n):
        return rc(ctx_h.at[:, :, cols_of(mine[n])], cbuf.at[n], out_sem.at[CX], cx_rs.at[n], peer)

    cxf = rc(inf_h, infx, out_sem.at[CXF], cx_rs.at[half], peer)

    def sub(core, u):
        return pl.ds(pl.multiple_of(core * R + u * S, S), S)

    def ag(d, s, u, shift):
        qq = chip_at(-sign[d] * (s - 1 + shift))
        dst = wb.at[qq, sub(c, u)]
        src = w_h.at[pl.ds(u * S, S)] if (s == 1 and shift == 0) else dst
        return rc(src, dst, out_sem.at[AG], ag_rs.at[2 * (s - 1) + int(u != d)], side[d])

    def pt(s, u, offset, own):
        qq = chip_at(offset)
        dst = wb.at[qq, sub(c if own else 1 - c, u)]
        src = w_h.at[pl.ds(u * S, S)] if (own and s == 0) else dst
        return rc(src, dst, out_sem.at[PT], pt_rs.at[s], partner)

    def both_wait(sems, i):
        held = wb.at[q, rows_of(c)]
        rc(held, held, out_sem.at[AG], sems.at[i], nxt).wait_recv()

    def pt_wait(s):
        held = wb.at[q] if 0 < s < far else wb.at[q, rows_of(c)]
        rc(held, held, out_sem.at[PT], pt_rs.at[s], partner).wait_recv()

    pl.semaphore_wait(barrier, len(greet))
    cxf.start()
    for n in range(half):
        cx(n).start()
    for t in range(2):
        for d in range(2):
            ag(d, 1, d if t == 0 else 1 - d, 0).start()
        pt(0, t, 0, True).start()

    ld_inf.wait()
    ld_ctx.wait()
    inw = inf[...].astype(F32)
    for e in range(E):
        v = (ctx[e].astype(F32) * inw[e:e + 1]).astype(BF16)
        for j in range(half):
            sc[m * half + j, e * T:(e + 1) * T, :] = v[:, j * R2:(j + 1) * R2]
    ld_outf.wait()
    ld_cot.wait()
    outw = outf[...].astype(F32)
    for e in range(E):
        sg[e * T:(e + 1) * T, :] = (cot[e].astype(F32) * outw[e:e + 1]).astype(BF16)

    def px(qq):
        return rc(part.at[qq], xrecv.at[qq % half], out_sem.at[PX], px_rs.at[qq % half], peer)

    def ps(qq):
        return rc(psend.at[qq], precv.at[qq], out_sem.at[PS], ps_rs.at[qq], partner)

    def gw_one(qq):
        g = lax.dot_general(sc[qq], sg[...], (((0,), (0,)), ((), ())), preferred_element_type=F32)
        gall[qq, 0] = g[:R]
        gall[qq, 1] = g[R:]
        psend[qq] = gall[qq, 1 - c].astype(BF16)
        ps(qq).start()

    def order_at(i):
        return chip_at((far - (i + 1) // 2) * (1 - 2 * ((i + 1) % 2)))

    def gw_mine():
        def body(i, carry):
            qq = order_at(i)

            @pl.when(qq // half == m)
            def _():
                gw_one(qq)
            return carry
        lax.fori_loop(0, C, body, 0)

    def project(qq):
        proj[...] += jnp.dot(sc[qq], wb[qq], preferred_element_type=F32)

    def process(offsets):
        def body(j, carry):
            off = offsets[0] if len(offsets) == 1 else offsets[0] + j * (offsets[1] - offsets[0])
            qq = chip_at(off)
            part[qq] = lax.dot_general(
                sg[...], wb[qq], (((1,), (1,)), ((), ())), preferred_element_type=F32
            ).astype(BF16)

            @pl.when(qq // half != m)
            def _():
                px(qq).start()

            @pl.when(qq // half == m)
            def _():
                project(qq)
            return carry
        lax.fori_loop(0, len(offsets), body, 0)

    def piece(k, u, d):
        return 2 * k - 1 + int(u == d) if k else 0

    def rs(d, k, u):
        i = piece(k, u, d)
        return rc(rsend.at[d, i], rrecv.at[d, i], out_sem.at[RS], rs_rs.at[i], side[d])

    def chip_sum(qq, u):
        rows = slice(u * S, (u + 1) * S)
        return gall[qq, c, rows, :] + precv[qq, rows, :].astype(F32)

    def rs_sub(k, late):
        chips = [chip_at(sign[d] * (far - k)) if k else chip_at(-far) for d in range(2)]
        if k == 0:
            ps(chips[0]).wait_recv()
        elif not late:
            for d in range(2):
                ps(chips[d]).wait_recv()
        held = k > 1 or (k == 1 and late)
        if held:
            both_wait(rs_rs, piece(k - 1, int(late), 1))
        for d in range(2):
            u = d if late else 1 - d
            v = chip_sum(chips[d], u)
            if held:
                v = v + rrecv[d, piece(k - 1, u, d)].astype(F32)
            rsend[d, piece(k, u, d)] = v.astype(BF16)
            rs(d, k, u).start()

    proj[...] = jnp.zeros(proj.shape, F32)
    gw_mine()
    ld_w.wait()
    pt_wait(0)
    process([0])

    def scale_in(n):
        cx(n).wait_recv()
        for e in range(E):
            wide = infx[e:e + 1, cols_of(theirs[n])].astype(F32)
            sc[theirs[n], e * T:(e + 1) * T, :] = (cbuf[n, e].astype(F32) * wide).astype(BF16)
        gw_one(theirs[n])

    def forward(s, t):
        both_wait(ag_rs, 2 * (s - 1) + t)
        for d in range(2):
            u = d if t == 0 else 1 - d
            if s + 1 < far or (s + 1 == far and t == 0):
                ag(d, s + 1, u, 0).start()
            pt(s, u, -sign[d] * s, True).start()

    for s in range(1, far):
        forward(s, 0)
        if s == far - 1:
            rs_sub(0, True)
        if s == 1:
            gr[...] = jnp.sum(cot[...].astype(F32), axis=0)
            store(1, gr, gr_o)
        else:
            pt_wait(s - 1)
            process([1 - s])
        forward(s, 1)
        if s > 1:
            process([s - 1])
            if s == 2:
                cxf.wait_recv()
            scale_in(s - 2)
    scale_in(far - 2)
    both_wait(ag_rs, 2 * (far - 1))
    for d in range(2):
        pt(far, d, far, True).start()
    pt_wait(far - 1)
    process([1 - far])
    rs_sub(1, False)
    process([far - 1])
    pt_wait(far)
    process([far])
    for n in range(far - 1):
        project(theirs[n])
    rs_sub(1, True)
    for n in range(far - 1, half):
        scale_in(n)
        project(theirs[n])

    ld_res.wait()
    resw = res[...].astype(F32)
    for e in range(E):
        pe = proj[e * T:(e + 1) * T, :]
        hid[e] = (resw + pe * outw[e:e + 1]).astype(BF16)
        a = jnp.sum(cot[e].astype(F32) * pe, axis=0, keepdims=True)
        for h in range(2):
            arb[h, 2 * E + e:2 * E + e + 1, :] = a[:, h * H2:(h + 1) * H2]
    store(0, hid, hid_o)
    for n in range(half):
        h, first = n * R2 // H2, n * R2 % H2
        slot = theirs[n] % half
        ahead = slot * R2 // H2
        far_cols = pl.ds(pl.multiple_of(slot * R2 - ahead * H2, R2), R2)
        for e in range(E):
            rows = slice(e * T, (e + 1) * T)
            a = ctx[e, :, n * R2:(n + 1) * R2].astype(F32) * part[m * half + n, rows, :].astype(F32)
            arb[h, e:e + 1, first:first + R2] = jnp.sum(a, axis=0, keepdims=True)
            a = cbuf[n, e].astype(F32) * part[theirs[n], rows, :].astype(F32)
            arb[ahead, E + e:E + e + 1, far_cols] = jnp.sum(a, axis=0, keepdims=True)

    def ar(i, src, dev):
        return rc(src, arr.at[i], out_sem.at[AR], ar_rs.at[min(i, 2)], dev)

    to_partner = ar(0, arb.at[1 - c], partner)
    to_beside = ar(1, ars.at[0], beside)
    to_lines = [ar(1 + i, ars.at[1], along(i)) for i in range(1, lines)]
    from_lines = rc(arr.at[2:], arr.at[2:], out_sem.at[AR], ar_rs.at[2], partner)
    all_sums = rc(arr, arr, out_sem.at[AR], ar_rs.at[2], partner)
    to_other = rc(fin.at[0], fin.at[1], out_sem.at[FIN], ar_rs.at[3], partner)
    swaps = [rc(swp, swr.at[c], out_sem.at[SWAP], ar_rs.at[4], dev) for dev in (peer, cross)]
    both_swaps = rc(swr, swr, out_sem.at[SWAP], ar_rs.at[4], peer)

    own_half = pl.ds(pl.multiple_of(c * H2, H2), H2)
    other_half = pl.ds(pl.multiple_of((1 - c) * H2, H2), H2)

    def ar_step(i):
        if i == 0:
            to_partner.wait_recv()
            ars[0] = arb[c] + arr[0]
            to_beside.start()
        elif i == 1:
            to_beside.wait_recv()
            ars[1] = ars[0] + arr[1]
            for copy in to_lines:
                copy.start()
        else:
            from_lines.wait_recv()
            total = ars[1]
            for n in range(2, lines + 1):
                total = total + arr[n]
            swp[...] = total[E:2 * E]
            fin[0, :E] = total[:E]
            fin[0, E:] = total[2 * E:]
            for copy in swaps:
                copy.start()
            to_other.start()

    def finish(n):
        chip = mine[n]
        slot = chip % half
        rc(xrecv.at[slot], xrecv.at[slot], out_sem.at[PX], px_rs.at[slot], peer).wait_recv()
        for e in range(E):
            rows = slice(e * T, (e + 1) * T)
            be = part[chip, rows, :].astype(F32) + xrecv[slot, rows, :].astype(F32)
            wide = inf[e:e + 1, cols_of(chip)].astype(F32)
            gc[e, :, cols_of(chip)] = (be * wide).astype(BF16)
        store(2, gc.at[:, :, cols_of(chip)], gc_o.at[:, :, cols_of(chip)])

    to_partner.start()
    pending = half
    for k in range(2, far):
        rs_sub(k, False)
        if k == 2:
            ar_step(0)
        rs_sub(k, True)
        if k == 2:
            ar_step(1)
        if pending > 2:
            pending -= 1
            finish(pending)
    ar_step(2)
    ps(q).wait_recv()
    for t in range(2):
        both_wait(rs_rs, piece(far - 1, t, 1))
    for u in range(2):
        rows = slice(u * S, (u + 1) * S)
        total = chip_sum(q, u)
        for d in range(2):
            total = total + rrecv[d, piece(far - 1, u, d)].astype(F32)
        gw[rows, :] = total
        store(3, gw.at[pl.ds(u * S, S)], gw_o.at[pl.ds(u * S, S)])
    to_other.wait_recv()
    go[:, own_half] = fin[0, E:]
    go[:, other_half] = fin[1, E:]
    store(4, go, go_o)
    while pending > 0:
        pending -= 1
        finish(pending)
    both_swaps.wait_recv()
    gi[:, own_half] = fin[0, :E] + swr[c]
    gi[:, other_half] = fin[1, :E] + swr[1 - c]
    store(5, gi, gi_o)

    sent = (
        (CX, cbuf), (CXF, infx), (AG, rsend), (PT, psend), (PX, xrecv),
        (PS, psend), (RS, rsend), (AR, arr), (SWAP, swr), (FIN, fin.at[0]),
    )
    for i, ref in sent:
        rc(ref, ref, out_sem.at[i], ar_rs.at[4], peer).wait_send()
    stored = ((hid, hid_o), (gr, gr_o), (gc, gc_o), (gw, gw_o), (go, go_o), (gi, gi_o))
    for i, (src, dst) in enumerate(stored):
        pltpu.make_async_copy(src, dst, st_sem.at[i]).wait()


def fused(C, context, residual, out_weight, in_factor, out_factor, cotangent):
    E, T, H = context.shape
    M = E * T
    R = out_weight.shape[0]
    half = C // 2
    far = half
    lines = C // 2
    pieces = 2 * far - 1
    hbm = pl.BlockSpec(memory_space=pl.ANY)
    dma = pltpu.SemaphoreType.DMA
    shape = jax.ShapeDtypeStruct
    results = pl.pallas_call(
        functools.partial(kernel, C),
        out_shape=(
            pltpu.VMEM((E, T, H), BF16),
            pltpu.VMEM((E, T, H), BF16),
            pltpu.VMEM((R, H), F32),
            pltpu.VMEM((E, H), F32),
            pltpu.VMEM((E, H), F32),
            pltpu.VMEM((T, H), F32),
        ),
        in_specs=[hbm] * 6,
        out_specs=tuple([hbm] * 6),
        scratch_shapes=[
            pltpu.VMEM((E, T, H), BF16),
            pltpu.VMEM((E, T, H), BF16),
            pltpu.VMEM((R, H), F32),
            pltpu.VMEM((E, H), F32),
            pltpu.VMEM((E, H), F32),
            pltpu.VMEM((T, H), F32),
            pltpu.VMEM((E, T, H), BF16),
            pltpu.VMEM((E, T, H), BF16),
            pltpu.VMEM((T, H), BF16),
            pltpu.VMEM((E, H), BF16),
            pltpu.VMEM((E, H), BF16),
            pltpu.VMEM((half, E, T, 2 * R), BF16),
            pltpu.VMEM((E, H), BF16),
            pltpu.VMEM((C, M, 2 * R), BF16),
            pltpu.VMEM((M, H), BF16),
            pltpu.VMEM((C, 2 * R, H), BF16),
            pltpu.VMEM((M, H), F32),
            pltpu.VMEM((C, M, 2 * R), BF16),
            pltpu.VMEM((half, M, 2 * R), BF16),
            pltpu.VMEM((C, 2, R, H), F32),
            pltpu.VMEM((C, R, H), BF16),
            pltpu.VMEM((C, R, H), BF16),
            pltpu.VMEM((2, pieces, R // 2, H), BF16),
            pltpu.VMEM((2, pieces, R // 2, H), BF16),
            pltpu.VMEM((2, 3 * E, H // 2), F32),
            pltpu.VMEM((2, 3 * E, H // 2), F32),
            pltpu.VMEM((lines + 1, 3 * E, H // 2), F32),
            pltpu.VMEM((2, 2 * E, H // 2), F32),
            pltpu.VMEM((E, H // 2), F32),
            pltpu.VMEM((2, E, H // 2), F32),
            dma((6,)),
            dma((6,)),
            dma((10,)),
            dma((half + 1,)),
            dma((pieces,)),
            dma((far + 1,)),
            dma((half,)),
            dma((C,)),
            dma((pieces,)),
            dma((5,)),
        ],
        compiler_params=pltpu.CompilerParams(
            collective_id=0, has_side_effects=True, vmem_limit_bytes=62208 * 1024
        ),
    )(context, residual, out_weight, in_factor, out_factor, cotangent)
    return pl.pallas_call(
        deliver,
        out_shape=tuple(shape(r.shape, r.dtype) for r in results),
        in_specs=[hbm] * 6,
        out_specs=tuple([hbm] * 6),
        scratch_shapes=[dma((6,))],
        compiler_params=pltpu.CompilerParams(vmem_limit_bytes=1024 * 1024),
    )(*results)


def deliver(*refs):
    copies = [pltpu.make_async_copy(refs[i], refs[6 + i], refs[12].at[i]) for i in range(6)]
    for copy in copies:
        copy.start()
    for copy in copies:
        copy.wait()


def solution(mesh):
    in_specs = (
        P(None, "fsdp", "member"),
        P("fsdp", "member"),
        P("fsdp", "member"),
        P(None, "member"),
        P(None, "member"),
        P(None, "fsdp", "member"),
    )
    out_specs = (
        P(None, "fsdp", "member"),
        P(None, "fsdp", "member"),
        P("fsdp", "member"),
        P(None, "member"),
        P(None, "member"),
        P("fsdp", "member"),
    )
    members = mesh.shape["member"]
    chips = mesh.shape["fsdp"] // 2
    if members == 2 and chips >= 8 and chips & (chips - 1) == 0:
        per_device = functools.partial(fused, chips)
    else:
        per_device = general
    return jax.shard_map(
        per_device, mesh=mesh, in_specs=in_specs, out_specs=out_specs, check_vma=False
    )
```

```python
import functools

import jax
import jax.numpy as jnp
from jax import lax
from jax.experimental import pallas as pl
from jax.experimental.pallas import tpu as pltpu
from jax.sharding import PartitionSpec as P

F32 = jnp.float32
BF16 = jnp.bfloat16


def general(context, residual, out_weight, in_factor, out_factor, cotangent):
    in_wide = in_factor.astype(jnp.float32)
    out_wide = out_factor.astype(jnp.float32)
    scaled_local = (context.astype(jnp.float32) * in_wide[:, None, :]).astype(jnp.bfloat16)
    scaled_grad = (cotangent.astype(jnp.float32) * out_wide[:, None, :]).astype(jnp.bfloat16)
    scaled_context = lax.all_gather(scaled_local, "member", axis=2, tiled=True)
    weight = lax.all_gather(out_weight, "fsdp", axis=0, tiled=True)
    projected = jnp.einsum(
        "eti,id->etd", scaled_context, weight, preferred_element_type=jnp.float32
    )
    partial_value = jnp.einsum(
        "etd,id->eti", scaled_grad, weight, preferred_element_type=jnp.float32
    )
    hidden = (residual.astype(jnp.float32)[None] + projected * out_wide[:, None, :]).astype(
        jnp.bfloat16
    )
    backward = lax.psum_scatter(
        partial_value.astype(jnp.bfloat16), "member", scatter_dimension=2, tiled=True
    ).astype(jnp.float32)
    grad_context = (backward * in_wide[:, None, :]).astype(jnp.bfloat16)
    grad_in_local = jnp.sum(context.astype(jnp.float32) * backward, axis=1)
    grad_out_local = jnp.sum(cotangent.astype(jnp.float32) * projected, axis=1)
    grad_in, grad_out = lax.psum((grad_in_local, grad_out_local), "fsdp")
    grad_block = jnp.einsum(
        "eti,etd->id", scaled_context, scaled_grad, preferred_element_type=jnp.float32
    )
    grad_weight = lax.psum_scatter(grad_block, "fsdp", scatter_dimension=0, tiled=True)
    grad_residual = jnp.sum(cotangent.astype(jnp.float32), axis=0)
    return (hidden, grad_context, grad_weight, grad_in, grad_out, grad_residual)


def kernel(
    C,
    ctx_h, res_h, w_h, inf_h, outf_h, cot_h,
    hid_o, gc_o, gw_o, gi_o, go_o, gr_o,
    hid, gc, gw, gi, go, gr,
    ctx, cot, res, inf, outf, cbuf, infx, sc, sg, wb, proj, part, xrecv, gall, psend, precv, rsend, rrecv,
    arb, ars, arr, fin, swp, swr,
    cx_rs, ag_rs, pt_rs, px_rs, ps_rs, rs_rs, ar_rs, ready,
):
    dma = pltpu.SemaphoreType.DMA
    pl.run_scoped(
        functools.partial(
            work, C,
            ctx_h, res_h, w_h, inf_h, outf_h, cot_h,
            hid_o, gc_o, gw_o, gi_o, go_o, gr_o,
            hid, gc, gw, gi, go, gr,
            ctx, cot, res, inf, outf, cbuf, infx, sc, sg, wb, proj, part, xrecv, gall, psend, precv, rsend, rrecv,
            arb, ars, arr, fin, swp, swr,
            cx_rs, ag_rs, pt_rs, px_rs, ps_rs, rs_rs, ar_rs, ready,
        ),
        dma((6,)), dma((6,)), dma((10,)),
    )


def work(
    C,
    ctx_h, res_h, w_h, inf_h, outf_h, cot_h,
    hid_o, gc_o, gw_o, gi_o, go_o, gr_o,
    hid, gc, gw, gi, go, gr,
    ctx, cot, res, inf, outf, cbuf, infx, sc, sg, wb, proj, part, xrecv, gall, psend, precv, rsend, rrecv,
    arb, ars, arr, fin, swp, swr,
    cx_rs, ag_rs, pt_rs, px_rs, ps_rs, rs_rs, ar_rs, ready,
    ld_sem, st_sem, out_sem,
):
    E, T, H = ctx.shape
    R = w_h.shape[0]
    R2 = 2 * R
    S = R // 2
    half = C // 2
    far = C // 2
    lines = C // 2
    H2 = H // 2
    pieces = 2 * far - 1

    m = lax.axis_index("member")
    f = lax.axis_index("fsdp")
    c = f % 2
    q = f // 2
    p = (1 - q % 2) * (q // 2) + (q % 2) * (C - 1 - q // 2)

    def chip_at(offset):
        pos = (p + offset + C) % C
        y = pos // half
        return 2 * ((1 - y) * pos + y * (C - 1 - pos)) + y

    peer = (1 - m, f)
    partner = (m, q * 2 + 1 - c)
    nxt = (m, chip_at(1) * 2 + c)
    prv = (m, chip_at(-1) * 2 + c)
    side = (nxt, prv)
    sign = (1, -1)
    cross = (1 - m, q * 2 + 1 - c)
    beside = (m, f + 2 - 4 * (q % 2))

    def along(i):
        line = q // 2
        other = 0
        bit = 1
        while bit < lines:
            own = (line // bit) % 2
            other = other + bit * (1 - own if i & bit else own)
            bit *= 2
        return (m, f + 4 * (other - line))


    def rc(src, dst, ss, rs, dev):
        return pltpu.make_async_remote_copy(
            src_ref=src, dst_ref=dst, send_sem=ss, recv_sem=rs,
            device_id=dev, device_id_type=pl.DeviceIdType.MESH,
        )

    barrier = pltpu.get_barrier_semaphore()

    def greet(dev):
        pl.semaphore_signal(barrier, inc=1, device_id=dev, device_id_type=pl.DeviceIdType.MESH)

    lead, deputy = m * (1 - c) == 1, m * c == 1
    greet((1 - m, q * 2 + m * c))

    @pl.when(jnp.logical_not(lead))
    def _():
        greet(partner)

    for ahead in (1, -1):
        greet((m, chip_at(ahead) * 2 + c + m * (1 - c)))

    def rows_of(core):
        return pl.ds(pl.multiple_of(core * R, R), R)

    def load(i, src, dst):
        copy = pltpu.make_async_copy(src, dst, ld_sem.at[i])
        copy.start()
        return copy

    def store(i, src, dst):
        pltpu.make_async_copy(src, dst, st_sem.at[i]).start()

    CX, CXF, AG, PT, PX, PS, RS, AR, SWAP, FIN = range(10)

    ld_inf = load(0, inf_h, inf)
    ld_ctx = load(1, ctx_h, ctx)
    ld_outf = load(2, outf_h, outf)
    ld_cot = load(3, cot_h, cot)
    ld_w = load(4, w_h, wb.at[q, rows_of(c)])
    ld_res = load(5, res_h, res)

    order = [chip_at(-far)] + [chip_at(s * (far - k)) for k in range(1, far) for s in sign] + [q]

    def ranked(side_of):
        found = [0] * half
        count = 0
        for chip in order:
            member = chip // half == side_of
            for n in range(half):
                found[n] = jnp.where(jnp.logical_and(member, count == n), chip, found[n])
            count = count + jnp.where(member, 1, 0)
        return found

    mine = ranked(m)
    theirs = ranked(1 - m)

    def cols_of(chip):
        return pl.ds(pl.multiple_of((chip % half) * R2, R2), R2)

    def cx(n):
        return rc(ctx_h.at[:, :, cols_of(mine[n])], cbuf.at[n], out_sem.at[CX], cx_rs.at[n], peer)

    cxf = rc(inf_h, infx, out_sem.at[CXF], cx_rs.at[half], peer)

    def sub(core, u):
        return pl.ds(pl.multiple_of(core * R + u * S, S), S)

    def ag(d, s, u, shift):
        qq = chip_at(-sign[d] * (s - 1 + shift))
        dst = wb.at[qq, sub(c, u)]
        src = w_h.at[pl.ds(u * S, S)] if (s == 1 and shift == 0) else dst
        return rc(src, dst, out_sem.at[AG], ag_rs.at[2 * (s - 1) + int(u != d)], side[d])

    def pt(s, u, offset, own):
        qq = chip_at(offset)
        dst = wb.at[qq, sub(c if own else 1 - c, u)]
        src = w_h.at[pl.ds(u * S, S)] if (own and s == 0) else dst
        return rc(src, dst, out_sem.at[PT], pt_rs.at[s], partner)

    def both_wait(sems, i):
        held = wb.at[q, rows_of(c)]
        rc(held, held, out_sem.at[AG], sems.at[i], nxt).wait_recv()

    def pt_wait(s):
        held = wb.at[q] if 0 < s < far else wb.at[q, rows_of(c)]
        rc(held, held, out_sem.at[PT], pt_rs.at[s], partner).wait_recv()

    def tell(sem):
        pl.semaphore_signal(sem, inc=1, device_id=partner, device_id_type=pl.DeviceIdType.MESH)

    @pl.when(jnp.logical_not(deputy))
    def _():
        pl.semaphore_wait(barrier, 4 - m)

    @pl.when(lead)
    def _():
        tell(ready)

    @pl.when(deputy)
    def _():
        pl.semaphore_wait(ready, 1)

    cxf.start()
    for n in range(half):
        cx(n).start()

    @pl.when(deputy)
    def _():
        pl.semaphore_wait(barrier, 4)
        tell(ready)

    @pl.when(lead)
    def _():
        pl.semaphore_wait(ready, 1)

    for t in range(2):
        for d in range(2):
            ag(d, 1, d if t == 0 else 1 - d, 0).start()
        pt(0, t, 0, True).start()

    ld_inf.wait()
    ld_ctx.wait()
    inw = inf[...].astype(F32)
    for e in range(E):
        v = (ctx[e].astype(F32) * inw[e:e + 1]).astype(BF16)
        for j in range(half):
            sc[m * half + j, e * T:(e + 1) * T, :] = v[:, j * R2:(j + 1) * R2]
    ld_outf.wait()
    ld_cot.wait()
    outw = outf[...].astype(F32)
    for e in range(E):
        sg[e * T:(e + 1) * T, :] = (cot[e].astype(F32) * outw[e:e + 1]).astype(BF16)

    def px(qq, first):
        rows = pl.ds(0 if first else E * T // 2, E * T // 2)
        return rc(part.at[qq, rows], xrecv.at[qq % half, rows], out_sem.at[PX], px_rs.at[qq % half], peer)

    def ps(qq):
        return rc(psend.at[qq], precv.at[qq], out_sem.at[PS], ps_rs.at[qq], partner)

    def gw_one(qq):
        g = lax.dot_general(sc[qq], sg[...], (((0,), (0,)), ((), ())), preferred_element_type=F32)
        gall[qq, 0] = g[:R]
        gall[qq, 1] = g[R:]
        psend[qq] = gall[qq, 1 - c].astype(BF16)
        ps(qq).start()

    def order_at(i):
        return chip_at((far - (i + 1) // 2) * (1 - 2 * ((i + 1) % 2)))

    def gw_mine():
        def body(i, carry):
            qq = order_at(i)

            @pl.when(qq // half == m)
            def _():
                gw_one(qq)
            return carry
        lax.fori_loop(0, C, body, 0)

    def project(qq):
        proj[...] += jnp.dot(sc[qq], wb[qq], preferred_element_type=F32)

    def process(offsets):
        def body(j, carry):
            off = offsets[0] if len(offsets) == 1 else offsets[0] + j * (offsets[1] - offsets[0])
            qq = chip_at(off)
            part[qq] = lax.dot_general(
                sg[...], wb[qq], (((1,), (1,)), ((), ())), preferred_element_type=F32
            ).astype(BF16)

            @pl.when(qq // half != m)
            def _():
                px(qq, True).start()

            @pl.when(jnp.logical_and(qq // half != m, qq != theirs[0]))
            def _():
                px(qq, False).start()

            @pl.when(qq // half == m)
            def _():
                project(qq)
            return carry
        lax.fori_loop(0, len(offsets), body, 0)

    def piece(k, u, d):
        return 2 * k - 1 + int(u == d) if k else 0

    def rs(d, k, u):
        i = piece(k, u, d)
        return rc(rsend.at[d, i], rrecv.at[d, i], out_sem.at[RS], rs_rs.at[i], side[d])

    def chip_sum(qq, u):
        rows = slice(u * S, (u + 1) * S)
        return gall[qq, c, rows, :] + precv[qq, rows, :].astype(F32)

    def rs_sub(k, late):
        chips = [chip_at(sign[d] * (far - k)) if k else chip_at(-far) for d in range(2)]
        if k == 0:
            ps(chips[0]).wait_recv()
        elif not late:
            for d in range(2):
                ps(chips[d]).wait_recv()
        held = k > 1 or (k == 1 and late)
        if held:
            both_wait(rs_rs, piece(k - 1, int(late), 1))
        for d in range(2):
            u = d if late else 1 - d
            v = chip_sum(chips[d], u)
            if held:
                v = v + rrecv[d, piece(k - 1, u, d)].astype(F32)
            rsend[d, piece(k, u, d)] = v.astype(BF16)
            rs(d, k, u).start()

    proj[...] = jnp.zeros(proj.shape, F32)
    gw_mine()
    ld_w.wait()
    pt_wait(0)
    process([0])

    def scale_in(n):
        cx(n).wait_recv()
        for e in range(E):
            wide = infx[e:e + 1, cols_of(theirs[n])].astype(F32)
            sc[theirs[n], e * T:(e + 1) * T, :] = (cbuf[n, e].astype(F32) * wide).astype(BF16)
        gw_one(theirs[n])

    def forward(s, t):
        both_wait(ag_rs, 2 * (s - 1) + t)
        for d in range(2):
            u = d if t == 0 else 1 - d
            if s + 1 < far or (s + 1 == far and t == 0):
                ag(d, s + 1, u, 0).start()
            pt(s, u, -sign[d] * s, True).start()

    for s in range(1, far):
        forward(s, 0)
        if s == far - 1:
            rs_sub(0, True)
        if s == 1:
            gr[...] = jnp.sum(cot[...].astype(F32), axis=0)
            store(1, gr, gr_o)
        else:
            pt_wait(s - 1)
            process([1 - s])
        forward(s, 1)
        if s > 1:
            process([s - 1])
            if s == 2:
                cxf.wait_recv()
            scale_in(s - 2)
    scale_in(far - 2)
    both_wait(ag_rs, 2 * (far - 1))
    for d in range(2):
        pt(far, d, far, True).start()
    pt_wait(far - 1)
    process([1 - far])
    rs_sub(1, False)
    process([far - 1])
    pt_wait(far)
    process([far])
    for n in range(far - 1):
        project(theirs[n])
    rs_sub(1, True)
    for n in range(far - 1, half):
        scale_in(n)
        project(theirs[n])

    ld_res.wait()
    resw = res[...].astype(F32)
    for e in range(E):
        pe = proj[e * T:(e + 1) * T, :]
        hid[e] = (resw + pe * outw[e:e + 1]).astype(BF16)
        a = jnp.sum(cot[e].astype(F32) * pe, axis=0, keepdims=True)
        for h in range(2):
            arb[h, 2 * E + e:2 * E + e + 1, :] = a[:, h * H2:(h + 1) * H2]
    store(0, hid, hid_o)
    for n in range(half):
        h, first = n * R2 // H2, n * R2 % H2
        slot = theirs[n] % half
        ahead = slot * R2 // H2
        far_cols = pl.ds(pl.multiple_of(slot * R2 - ahead * H2, R2), R2)
        for e in range(E):
            rows = slice(e * T, (e + 1) * T)
            a = ctx[e, :, n * R2:(n + 1) * R2].astype(F32) * part[m * half + n, rows, :].astype(F32)
            arb[h, e:e + 1, first:first + R2] = jnp.sum(a, axis=0, keepdims=True)
            a = cbuf[n, e].astype(F32) * part[theirs[n], rows, :].astype(F32)
            arb[ahead, E + e:E + e + 1, far_cols] = jnp.sum(a, axis=0, keepdims=True)

    def ar(i, src, dev):
        return rc(src, arr.at[i], out_sem.at[AR], ar_rs.at[min(i, 2)], dev)

    to_partner = ar(0, arb.at[1 - c], partner)
    to_beside = ar(1, ars.at[0], beside)
    to_lines = [ar(1 + i, ars.at[1], along(i)) for i in range(1, lines)]
    from_lines = rc(arr.at[2:], arr.at[2:], out_sem.at[AR], ar_rs.at[2], partner)
    to_other = rc(fin.at[0], fin.at[1], out_sem.at[FIN], ar_rs.at[3], partner)
    swaps = [rc(swp, swr.at[c], out_sem.at[SWAP], ar_rs.at[4], dev) for dev in (peer, cross)]
    both_swaps = rc(swr, swr, out_sem.at[SWAP], ar_rs.at[4], peer)

    own_half = pl.ds(pl.multiple_of(c * H2, H2), H2)
    other_half = pl.ds(pl.multiple_of((1 - c) * H2, H2), H2)

    def ar_step(i):
        if i == 0:
            to_partner.wait_recv()
            ars[0] = arb[c] + arr[0]
            to_beside.start()
        elif i == 1:
            to_beside.wait_recv()
            ars[1] = ars[0] + arr[1]
            for copy in to_lines:
                copy.start()
        else:
            from_lines.wait_recv()
            total = ars[1]
            for n in range(2, lines + 1):
                total = total + arr[n]
            swp[...] = total[E:2 * E]
            fin[0, :E] = total[:E]
            fin[0, E:] = total[2 * E:]
            for copy in swaps:
                copy.start()
            to_other.start()

    def finish(n):
        chip = mine[n]
        slot = chip % half
        rc(xrecv.at[slot], xrecv.at[slot], out_sem.at[PX], px_rs.at[slot], peer).wait_recv()
        for e in range(E):
            rows = slice(e * T, (e + 1) * T)
            be = part[chip, rows, :].astype(F32) + xrecv[slot, rows, :].astype(F32)
            wide = inf[e:e + 1, cols_of(chip)].astype(F32)
            gc[e, :, cols_of(chip)] = (be * wide).astype(BF16)
        store(2, gc.at[:, :, cols_of(chip)], gc_o.at[:, :, cols_of(chip)])

    to_partner.start()
    pending = half
    for k in range(2, far):
        rs_sub(k, False)
        if k == 2:
            ar_step(0)
        rs_sub(k, True)
        if k == 2:
            ar_step(1)
        if pending > 2:
            pending -= 1
            finish(pending)
    ar_step(2)
    px(theirs[0], False).start()
    ps(q).wait_recv()
    for t in range(2):
        both_wait(rs_rs, piece(far - 1, t, 1))
    for u in range(2):
        rows = slice(u * S, (u + 1) * S)
        total = chip_sum(q, u)
        for d in range(2):
            total = total + rrecv[d, piece(far - 1, u, d)].astype(F32)
        gw[rows, :] = total
        store(3, gw.at[pl.ds(u * S, S)], gw_o.at[pl.ds(u * S, S)])
    to_other.wait_recv()
    go[:, own_half] = fin[0, E:]
    go[:, other_half] = fin[1, E:]
    store(4, go, go_o)
    while pending > 0:
        pending -= 1
        finish(pending)
    both_swaps.wait_recv()
    gi[:, own_half] = fin[0, :E] + swr[c]
    gi[:, other_half] = fin[1, :E] + swr[1 - c]
    store(5, gi, gi_o)

    sent = (
        (CX, cbuf), (CXF, infx), (AG, rsend), (PT, psend), (PX, xrecv),
        (PS, psend), (RS, rsend), (AR, arr), (SWAP, swr), (FIN, fin.at[0]),
    )
    for i, ref in sent:
        rc(ref, ref, out_sem.at[i], ar_rs.at[4], peer).wait_send()
    stored = ((hid, hid_o), (gr, gr_o), (gc, gc_o), (gw, gw_o), (go, go_o), (gi, gi_o))
    for i, (src, dst) in enumerate(stored):
        pltpu.make_async_copy(src, dst, st_sem.at[i]).wait()


def fused(C, context, residual, out_weight, in_factor, out_factor, cotangent):
    E, T, H = context.shape
    M = E * T
    R = out_weight.shape[0]
    half = C // 2
    far = half
    lines = C // 2
    pieces = 2 * far - 1
    hbm = pl.BlockSpec(memory_space=pl.ANY)
    dma = pltpu.SemaphoreType.DMA
    shape = jax.ShapeDtypeStruct
    results = pl.pallas_call(
        functools.partial(kernel, C),
        out_shape=(
            pltpu.VMEM((E, T, H), BF16),
            pltpu.VMEM((E, T, H), BF16),
            pltpu.VMEM((R, H), F32),
            pltpu.VMEM((E, H), F32),
            pltpu.VMEM((E, H), F32),
            pltpu.VMEM((T, H), F32),
        ),
        in_specs=[hbm] * 6,
        out_specs=tuple([hbm] * 6),
        scratch_shapes=[
            pltpu.VMEM((E, T, H), BF16),
            pltpu.VMEM((E, T, H), BF16),
            pltpu.VMEM((R, H), F32),
            pltpu.VMEM((E, H), F32),
            pltpu.VMEM((E, H), F32),
            pltpu.VMEM((T, H), F32),
            pltpu.VMEM((E, T, H), BF16),
            pltpu.VMEM((E, T, H), BF16),
            pltpu.VMEM((T, H), BF16),
            pltpu.VMEM((E, H), BF16),
            pltpu.VMEM((E, H), BF16),
            pltpu.VMEM((half, E, T, 2 * R), BF16),
            pltpu.VMEM((E, H), BF16),
            pltpu.VMEM((C, M, 2 * R), BF16),
            pltpu.VMEM((M, H), BF16),
            pltpu.VMEM((C, 2 * R, H), BF16),
            pltpu.VMEM((M, H), F32),
            pltpu.VMEM((C, M, 2 * R), BF16),
            pltpu.VMEM((half, M, 2 * R), BF16),
            pltpu.VMEM((C, 2, R, H), F32),
            pltpu.VMEM((C, R, H), BF16),
            pltpu.VMEM((C, R, H), BF16),
            pltpu.VMEM((2, pieces, R // 2, H), BF16),
            pltpu.VMEM((2, pieces, R // 2, H), BF16),
            pltpu.VMEM((2, 3 * E, H // 2), F32),
            pltpu.VMEM((2, 3 * E, H // 2), F32),
            pltpu.VMEM((lines + 1, 3 * E, H // 2), F32),
            pltpu.VMEM((2, 2 * E, H // 2), F32),
            pltpu.VMEM((E, H // 2), F32),
            pltpu.VMEM((2, E, H // 2), F32),
            dma((half + 1,)),
            dma((pieces,)),
            dma((far + 1,)),
            dma((half,)),
            dma((C,)),
            dma((pieces,)),
            dma((5,)),
            pltpu.SemaphoreType.REGULAR,
        ],
        compiler_params=pltpu.CompilerParams(
            collective_id=0, has_side_effects=True, vmem_limit_bytes=62208 * 1024
        ),
    )(context, residual, out_weight, in_factor, out_factor, cotangent)
    return pl.pallas_call(
        deliver,
        out_shape=tuple(shape(r.shape, r.dtype) for r in results),
        in_specs=[hbm] * 6,
        out_specs=tuple([hbm] * 6),
        scratch_shapes=[dma((6,))],
        compiler_params=pltpu.CompilerParams(vmem_limit_bytes=1024 * 1024),
    )(*results)


def deliver(*refs):
    copies = [pltpu.make_async_copy(refs[i], refs[6 + i], refs[12].at[i]) for i in range(6)]
    for copy in copies:
        copy.start()
    for copy in copies:
        copy.wait()


def solution(mesh):
    in_specs = (
        P(None, "fsdp", "member"),
        P("fsdp", "member"),
        P("fsdp", "member"),
        P(None, "member"),
        P(None, "member"),
        P(None, "fsdp", "member"),
    )
    out_specs = (
        P(None, "fsdp", "member"),
        P(None, "fsdp", "member"),
        P("fsdp", "member"),
        P(None, "member"),
        P(None, "member"),
        P("fsdp", "member"),
    )
    members = mesh.shape["member"]
    chips = mesh.shape["fsdp"] // 2
    if members == 2 and chips >= 8 and chips & (chips - 1) == 0:
        per_device = functools.partial(fused, chips)
    else:
        per_device = general
    return jax.shard_map(
        per_device, mesh=mesh, in_specs=in_specs, out_specs=out_specs, check_vma=False
    )
```

```python
import functools

import jax
import jax.numpy as jnp
from jax import lax
from jax.experimental import pallas as pl
from jax.experimental.pallas import tpu as pltpu
from jax.sharding import PartitionSpec as P

F32 = jnp.float32
BF16 = jnp.bfloat16


def general(context, residual, out_weight, in_factor, out_factor, cotangent):
    in_wide = in_factor.astype(jnp.float32)
    out_wide = out_factor.astype(jnp.float32)
    scaled_local = (context.astype(jnp.float32) * in_wide[:, None, :]).astype(jnp.bfloat16)
    scaled_grad = (cotangent.astype(jnp.float32) * out_wide[:, None, :]).astype(jnp.bfloat16)
    scaled_context = lax.all_gather(scaled_local, "member", axis=2, tiled=True)
    weight = lax.all_gather(out_weight, "fsdp", axis=0, tiled=True)
    projected = jnp.einsum(
        "eti,id->etd", scaled_context, weight, preferred_element_type=jnp.float32
    )
    partial_value = jnp.einsum(
        "etd,id->eti", scaled_grad, weight, preferred_element_type=jnp.float32
    )
    hidden = (residual.astype(jnp.float32)[None] + projected * out_wide[:, None, :]).astype(
        jnp.bfloat16
    )
    backward = lax.psum_scatter(
        partial_value.astype(jnp.bfloat16), "member", scatter_dimension=2, tiled=True
    ).astype(jnp.float32)
    grad_context = (backward * in_wide[:, None, :]).astype(jnp.bfloat16)
    grad_in_local = jnp.sum(context.astype(jnp.float32) * backward, axis=1)
    grad_out_local = jnp.sum(cotangent.astype(jnp.float32) * projected, axis=1)
    grad_in, grad_out = lax.psum((grad_in_local, grad_out_local), "fsdp")
    grad_block = jnp.einsum(
        "eti,etd->id", scaled_context, scaled_grad, preferred_element_type=jnp.float32
    )
    grad_weight = lax.psum_scatter(grad_block, "fsdp", scatter_dimension=0, tiled=True)
    grad_residual = jnp.sum(cotangent.astype(jnp.float32), axis=0)
    return (hidden, grad_context, grad_weight, grad_in, grad_out, grad_residual)


def kernel(C, *refs):
    half = C // 2
    far = C // 2
    dma = pltpu.SemaphoreType.DMA
    pl.run_scoped(
        functools.partial(work, C, *refs),
        dma((6,)),
        dma((6,)),
        dma((10,)),
        dma((half + 1,)),
        dma((2 * far - 1,)),
        dma((far + 1,)),
        dma((half + 1,)),
        dma((C,)),
        dma((2 * far - 1,)),
        dma((5,)),
        pltpu.SemaphoreType.REGULAR,
    )


def work(
    C,
    ctx_h, res_h, w_h, inf_h, outf_h, cot_h,
    hid_o, gc_o, gw_o, gi_o, go_o, gr_o,
    hid, gc, gw, gi, go, gr,
    ctx, cot, res, inf, outf, cbuf, infx, sc, sg, wb, proj, part, xrecv, gall, psend, precv, rsend, rrecv,
    arb, ars, arr, fin, swp, swr,
    ld_sem, st_sem, out_sem, cx_rs, ag_rs, pt_rs, px_rs, ps_rs, rs_rs, ar_rs, ready,
):
    E, T, H = ctx.shape
    R = w_h.shape[0]
    R2 = 2 * R
    S = R // 2
    half = C // 2
    far = C // 2
    lines = C // 2
    H2 = H // 2
    pieces = 2 * far - 1

    m = lax.axis_index("member")
    f = lax.axis_index("fsdp")
    c = f % 2
    q = f // 2
    p = (1 - q % 2) * (q // 2) + (q % 2) * (C - 1 - q // 2)

    def chip_at(offset):
        pos = (p + offset + C) % C
        y = pos // half
        return 2 * ((1 - y) * pos + y * (C - 1 - pos)) + y

    peer = (1 - m, f)
    partner = (m, q * 2 + 1 - c)
    nxt = (m, chip_at(1) * 2 + c)
    prv = (m, chip_at(-1) * 2 + c)
    side = (nxt, prv)
    sign = (1, -1)
    cross = (1 - m, q * 2 + 1 - c)
    beside = (m, f + 2 - 4 * (q % 2))

    def along(i):
        line = q // 2
        other = 0
        bit = 1
        while bit < lines:
            own = (line // bit) % 2
            other = other + bit * (1 - own if i & bit else own)
            bit *= 2
        return (m, f + 4 * (other - line))


    def rc(src, dst, ss, rs, dev):
        return pltpu.make_async_remote_copy(
            src_ref=src, dst_ref=dst, send_sem=ss, recv_sem=rs,
            device_id=dev, device_id_type=pl.DeviceIdType.MESH,
        )

    barrier = pltpu.get_barrier_semaphore()

    def greet(dev):
        pl.semaphore_signal(barrier, inc=1, device_id=dev, device_id_type=pl.DeviceIdType.MESH)

    lead, deputy = m * (1 - c) == 1, m * c == 1
    greet((1 - m, q * 2 + m * c))

    @pl.when(jnp.logical_not(lead))
    def _():
        greet(partner)

    for ahead in (1, -1):
        greet((m, chip_at(ahead) * 2 + c + m * (1 - c)))

    def rows_of(core):
        return pl.ds(pl.multiple_of(core * R, R), R)

    def load(i, src, dst):
        copy = pltpu.make_async_copy(src, dst, ld_sem.at[i])
        copy.start()
        return copy

    def store(i, src, dst):
        pltpu.make_async_copy(src, dst, st_sem.at[i]).start()

    CX, CXF, AG, PT, PX, PS, RS, AR, SWAP, FIN = range(10)

    ld_inf = load(0, inf_h, inf)
    ld_ctx = load(1, ctx_h, ctx)
    ld_outf = load(2, outf_h, outf)
    ld_cot = load(3, cot_h, cot)
    ld_w = load(4, w_h, wb.at[q, rows_of(c)])
    ld_res = load(5, res_h, res)

    order = [chip_at(-far)] + [chip_at(s * (far - k)) for k in range(1, far) for s in sign] + [q]

    def ranked(side_of):
        found = [0] * half
        count = 0
        for chip in order:
            member = chip // half == side_of
            for n in range(half):
                found[n] = jnp.where(jnp.logical_and(member, count == n), chip, found[n])
            count = count + jnp.where(member, 1, 0)
        return found

    mine = ranked(m)
    theirs = ranked(1 - m)

    def cols_of(chip):
        return pl.ds(pl.multiple_of((chip % half) * R2, R2), R2)

    def cx(n):
        return rc(ctx_h.at[:, :, cols_of(mine[n])], cbuf.at[n], out_sem.at[CX], cx_rs.at[n], peer)

    cxf = rc(inf_h, infx, out_sem.at[CXF], cx_rs.at[half], peer)

    def sub(core, u):
        return pl.ds(pl.multiple_of(core * R + u * S, S), S)

    def ag(d, s, u, shift):
        qq = chip_at(-sign[d] * (s - 1 + shift))
        dst = wb.at[qq, sub(c, u)]
        src = w_h.at[pl.ds(u * S, S)] if (s == 1 and shift == 0) else dst
        return rc(src, dst, out_sem.at[AG], ag_rs.at[2 * (s - 1) + int(u != d)], side[d])

    def pt(s, u, offset, own):
        qq = chip_at(offset)
        dst = wb.at[qq, sub(c if own else 1 - c, u)]
        src = w_h.at[pl.ds(u * S, S)] if (own and s == 0) else dst
        return rc(src, dst, out_sem.at[PT], pt_rs.at[s], partner)

    def both_wait(sems, i):
        held = wb.at[q, rows_of(c)]
        rc(held, held, out_sem.at[AG], sems.at[i], nxt).wait_recv()

    def pt_wait(s):
        held = wb.at[q] if 0 < s < far else wb.at[q, rows_of(c)]
        rc(held, held, out_sem.at[PT], pt_rs.at[s], partner).wait_recv()

    def tell(sem):
        pl.semaphore_signal(sem, inc=1, device_id=partner, device_id_type=pl.DeviceIdType.MESH)

    @pl.when(jnp.logical_not(deputy))
    def _():
        pl.semaphore_wait(barrier, 4 - m)

    @pl.when(lead)
    def _():
        tell(ready)

    @pl.when(deputy)
    def _():
        pl.semaphore_wait(ready, 1)

    cxf.start()
    for n in range(half):
        cx(n).start()

    @pl.when(deputy)
    def _():
        pl.semaphore_wait(barrier, 4)
        tell(ready)

    @pl.when(lead)
    def _():
        pl.semaphore_wait(ready, 1)

    for t in range(2):
        for d in range(2):
            ag(d, 1, d if t == 0 else 1 - d, 0).start()
        pt(0, t, 0, True).start()

    ld_inf.wait()
    ld_ctx.wait()
    inw = inf[...].astype(F32)
    for e in range(E):
        v = (ctx[e].astype(F32) * inw[e:e + 1]).astype(BF16)
        for j in range(half):
            sc[m * half + j, e * T:(e + 1) * T, :] = v[:, j * R2:(j + 1) * R2]
    ld_outf.wait()
    ld_cot.wait()
    outw = outf[...].astype(F32)
    for e in range(E):
        sg[e * T:(e + 1) * T, :] = (cot[e].astype(F32) * outw[e:e + 1]).astype(BF16)

    def px(qq, first, last=False):
        rows = pl.ds(0 if first else E * T // 2, E * T // 2)
        i = half if last else qq % half
        return rc(part.at[qq, rows], xrecv.at[qq % half, rows], out_sem.at[PX], px_rs.at[i], peer)

    def ps(qq):
        return rc(psend.at[qq], precv.at[qq], out_sem.at[PS], ps_rs.at[qq], partner)

    def gw_one(qq):
        g = lax.dot_general(sc[qq], sg[...], (((0,), (0,)), ((), ())), preferred_element_type=F32)
        gall[qq, 0] = g[:R]
        gall[qq, 1] = g[R:]
        psend[qq] = gall[qq, 1 - c].astype(BF16)
        ps(qq).start()

    def order_at(i):
        return chip_at((far - (i + 1) // 2) * (1 - 2 * ((i + 1) % 2)))

    def gw_mine():
        def body(i, carry):
            qq = order_at(i)

            @pl.when(qq // half == m)
            def _():
                gw_one(qq)
            return carry
        lax.fori_loop(0, C, body, 0)

    def project(qq):
        proj[...] += jnp.dot(sc[qq], wb[qq], preferred_element_type=F32)

    def process(offsets):
        def body(j, carry):
            off = offsets[0] if len(offsets) == 1 else offsets[0] + j * (offsets[1] - offsets[0])
            qq = chip_at(off)
            part[qq] = lax.dot_general(
                sg[...], wb[qq], (((1,), (1,)), ((), ())), preferred_element_type=F32
            ).astype(BF16)

            @pl.when(qq // half != m)
            def _():
                px(qq, True).start()

            @pl.when(jnp.logical_and(qq // half != m, qq != theirs[0]))
            def _():
                px(qq, False).start()

            @pl.when(qq // half == m)
            def _():
                project(qq)
            return carry
        lax.fori_loop(0, len(offsets), body, 0)

    def piece(k, u, d):
        return 2 * k - 1 + int(u == d) if k else 0

    def rs(d, k, u):
        i = piece(k, u, d)
        return rc(rsend.at[d, i], rrecv.at[d, i], out_sem.at[RS], rs_rs.at[i], side[d])

    def chip_sum(qq, u):
        rows = slice(u * S, (u + 1) * S)
        return gall[qq, c, rows, :] + precv[qq, rows, :].astype(F32)

    def rs_sub(k, late):
        chips = [chip_at(sign[d] * (far - k)) if k else chip_at(-far) for d in range(2)]
        if k == 0:
            ps(chips[0]).wait_recv()
        elif not late:
            for d in range(2):
                ps(chips[d]).wait_recv()
        held = k > 1 or (k == 1 and late)
        if held:
            both_wait(rs_rs, piece(k - 1, int(late), 1))
        for d in range(2):
            u = d if late else 1 - d
            v = chip_sum(chips[d], u)
            if held:
                v = v + rrecv[d, piece(k - 1, u, d)].astype(F32)
            rsend[d, piece(k, u, d)] = v.astype(BF16)
            rs(d, k, u).start()

    proj[...] = jnp.zeros(proj.shape, F32)
    gw_mine()
    ld_w.wait()
    pt_wait(0)
    process([0])

    def scale_in(n):
        cx(n).wait_recv()
        for e in range(E):
            wide = infx[e:e + 1, cols_of(theirs[n])].astype(F32)
            sc[theirs[n], e * T:(e + 1) * T, :] = (cbuf[n, e].astype(F32) * wide).astype(BF16)
        gw_one(theirs[n])

    def forward(s, t):
        both_wait(ag_rs, 2 * (s - 1) + t)
        for d in range(2):
            u = d if t == 0 else 1 - d
            if s + 1 < far or (s + 1 == far and t == 0):
                ag(d, s + 1, u, 0).start()
            pt(s, u, -sign[d] * s, True).start()

    for s in range(1, far):
        forward(s, 0)
        if s == far - 1:
            rs_sub(0, True)
        if s == 1:
            gr[...] = jnp.sum(cot[...].astype(F32), axis=0)
            store(1, gr, gr_o)
        else:
            pt_wait(s - 1)
            process([1 - s])
        forward(s, 1)
        if s > 1:
            process([s - 1])
            if s == 2:
                cxf.wait_recv()
            scale_in(s - 2)
    scale_in(far - 2)
    both_wait(ag_rs, 2 * (far - 1))
    for d in range(2):
        pt(far, d, far, True).start()
    pt_wait(far - 1)
    process([1 - far])
    rs_sub(1, False)
    process([far - 1])
    pt_wait(far)
    process([far])
    for n in range(far - 1):
        project(theirs[n])
    rs_sub(1, True)
    for n in range(far - 1, half):
        scale_in(n)
        project(theirs[n])

    ld_res.wait()
    resw = res[...].astype(F32)
    for e in range(E):
        pe = proj[e * T:(e + 1) * T, :]
        hid[e] = (resw + pe * outw[e:e + 1]).astype(BF16)
        a = jnp.sum(cot[e].astype(F32) * pe, axis=0, keepdims=True)
        for h in range(2):
            arb[h, 2 * E + e:2 * E + e + 1, :] = a[:, h * H2:(h + 1) * H2]
    store(0, hid, hid_o)
    for n in range(half):
        h, first = n * R2 // H2, n * R2 % H2
        slot = theirs[n] % half
        ahead = slot * R2 // H2
        far_cols = pl.ds(pl.multiple_of(slot * R2 - ahead * H2, R2), R2)
        for e in range(E):
            rows = slice(e * T, (e + 1) * T)
            a = ctx[e, :, n * R2:(n + 1) * R2].astype(F32) * part[m * half + n, rows, :].astype(F32)
            arb[h, e:e + 1, first:first + R2] = jnp.sum(a, axis=0, keepdims=True)
            a = cbuf[n, e].astype(F32) * part[theirs[n], rows, :].astype(F32)
            arb[ahead, E + e:E + e + 1, far_cols] = jnp.sum(a, axis=0, keepdims=True)

    def ar(i, src, dev):
        return rc(src, arr.at[i], out_sem.at[AR], ar_rs.at[min(i, 2)], dev)

    to_partner = ar(0, arb.at[1 - c], partner)
    to_beside = ar(1, ars.at[0], beside)
    to_lines = [ar(1 + i, ars.at[1], along(i)) for i in range(1, lines)]
    from_lines = rc(arr.at[2:], arr.at[2:], out_sem.at[AR], ar_rs.at[2], partner)
    to_other = rc(fin.at[0], fin.at[1], out_sem.at[FIN], ar_rs.at[3], partner)
    swaps = [rc(swp, swr.at[c], out_sem.at[SWAP], ar_rs.at[4], dev) for dev in (peer, cross)]
    both_swaps = rc(swr, swr, out_sem.at[SWAP], ar_rs.at[4], peer)

    own_half = pl.ds(pl.multiple_of(c * H2, H2), H2)
    other_half = pl.ds(pl.multiple_of((1 - c) * H2, H2), H2)

    def ar_step(i):
        if i == 0:
            to_partner.wait_recv()
            ars[0] = arb[c] + arr[0]
            to_beside.start()
        elif i == 1:
            to_beside.wait_recv()
            ars[1] = ars[0] + arr[1]
            for copy in to_lines:
                copy.start()
        else:
            from_lines.wait_recv()
            total = ars[1]
            for n in range(2, lines + 1):
                total = total + arr[n]
            swp[...] = total[E:2 * E]
            fin[0, :E] = total[:E]
            fin[0, E:] = total[2 * E:]
            for copy in swaps:
                copy.start()
            to_other.start()

    def finish(n, members, i):
        chip = mine[n]
        slot = chip % half
        held = xrecv.at[slot, pl.ds(members[0] * T, len(members) * T)]
        rc(held, held, out_sem.at[PX], px_rs.at[i], peer).wait_recv()
        for e in members:
            rows = slice(e * T, (e + 1) * T)
            be = part[chip, rows, :].astype(F32) + xrecv[slot, rows, :].astype(F32)
            wide = inf[e:e + 1, cols_of(chip)].astype(F32)
            gc[e, :, cols_of(chip)] = (be * wide).astype(BF16)
        rows = pl.ds(members[0], len(members))
        store(2, gc.at[rows, :, cols_of(chip)], gc_o.at[rows, :, cols_of(chip)])

    every = range(E)

    to_partner.start()
    pending = half
    for k in range(2, far):
        rs_sub(k, False)
        if k == 2:
            ar_step(0)
        rs_sub(k, True)
        if k == 2:
            ar_step(1)
        if pending > 2:
            pending -= 1
            finish(pending, every, mine[pending] % half)
    ar_step(2)
    px(theirs[0], False, True).start()
    ps(q).wait_recv()
    for t in range(2):
        both_wait(rs_rs, piece(far - 1, t, 1))
    for u in range(2):
        rows = slice(u * S, (u + 1) * S)
        total = chip_sum(q, u)
        for d in range(2):
            total = total + rrecv[d, piece(far - 1, u, d)].astype(F32)
        gw[rows, :] = total
        store(3, gw.at[pl.ds(u * S, S)], gw_o.at[pl.ds(u * S, S)])
    to_other.wait_recv()
    go[:, own_half] = fin[0, E:]
    go[:, other_half] = fin[1, E:]
    store(4, go, go_o)
    while pending > 1:
        pending -= 1
        finish(pending, every, mine[pending] % half)
    finish(0, every[:E // 2], mine[0] % half)
    finish(0, every[E // 2:], half)
    both_swaps.wait_recv()
    gi[:, own_half] = fin[0, :E] + swr[c]
    gi[:, other_half] = fin[1, :E] + swr[1 - c]
    store(5, gi, gi_o)

    sent = (
        (CX, cbuf), (CXF, infx), (AG, rsend), (PT, psend), (PX, xrecv),
        (PS, psend), (RS, rsend), (AR, arr), (SWAP, swr), (FIN, fin.at[0]),
    )
    for i, ref in sent:
        rc(ref, ref, out_sem.at[i], ar_rs.at[4], peer).wait_send()
    stored = ((hid, hid_o), (gr, gr_o), (gc, gc_o), (gw, gw_o), (go, go_o), (gi, gi_o))
    for i, (src, dst) in enumerate(stored):
        pltpu.make_async_copy(src, dst, st_sem.at[i]).wait()


def fused(C, context, residual, out_weight, in_factor, out_factor, cotangent):
    E, T, H = context.shape
    M = E * T
    R = out_weight.shape[0]
    half = C // 2
    far = half
    lines = C // 2
    pieces = 2 * far - 1
    hbm = pl.BlockSpec(memory_space=pl.ANY)
    shape = jax.ShapeDtypeStruct
    results = pl.pallas_call(
        functools.partial(kernel, C),
        out_shape=(
            pltpu.VMEM((E, T, H), BF16),
            pltpu.VMEM((E, T, H), BF16),
            pltpu.VMEM((R, H), F32),
            pltpu.VMEM((E, H), F32),
            pltpu.VMEM((E, H), F32),
            pltpu.VMEM((T, H), F32),
        ),
        in_specs=[hbm] * 6,
        out_specs=tuple([hbm] * 6),
        scratch_shapes=[
            pltpu.VMEM((E, T, H), BF16),
            pltpu.VMEM((E, T, H), BF16),
            pltpu.VMEM((R, H), F32),
            pltpu.VMEM((E, H), F32),
            pltpu.VMEM((E, H), F32),
            pltpu.VMEM((T, H), F32),
            pltpu.VMEM((E, T, H), BF16),
            pltpu.VMEM((E, T, H), BF16),
            pltpu.VMEM((T, H), BF16),
            pltpu.VMEM((E, H), BF16),
            pltpu.VMEM((E, H), BF16),
            pltpu.VMEM((half, E, T, 2 * R), BF16),
            pltpu.VMEM((E, H), BF16),
            pltpu.VMEM((C, M, 2 * R), BF16),
            pltpu.VMEM((M, H), BF16),
            pltpu.VMEM((C, 2 * R, H), BF16),
            pltpu.VMEM((M, H), F32),
            pltpu.VMEM((C, M, 2 * R), BF16),
            pltpu.VMEM((half, M, 2 * R), BF16),
            pltpu.VMEM((C, 2, R, H), F32),
            pltpu.VMEM((C, R, H), BF16),
            pltpu.VMEM((C, R, H), BF16),
            pltpu.VMEM((2, pieces, R // 2, H), BF16),
            pltpu.VMEM((2, pieces, R // 2, H), BF16),
            pltpu.VMEM((2, 3 * E, H // 2), F32),
            pltpu.VMEM((2, 3 * E, H // 2), F32),
            pltpu.VMEM((lines + 1, 3 * E, H // 2), F32),
            pltpu.VMEM((2, 2 * E, H // 2), F32),
            pltpu.VMEM((E, H // 2), F32),
            pltpu.VMEM((2, E, H // 2), F32),
        ],
        compiler_params=pltpu.CompilerParams(
            collective_id=0, has_side_effects=True, vmem_limit_bytes=62208 * 1024
        ),
    )(context, residual, out_weight, in_factor, out_factor, cotangent)
    return pl.pallas_call(
        deliver,
        out_shape=tuple(shape(r.shape, r.dtype) for r in results),
        in_specs=[hbm] * 6,
        out_specs=tuple([hbm] * 6),
        compiler_params=pltpu.CompilerParams(vmem_limit_bytes=1024 * 1024),
    )(*results)


def deliver(*refs):
    def run(sem):
        copies = [pltpu.make_async_copy(refs[i], refs[6 + i], sem.at[i]) for i in range(6)]
        for copy in copies:
            copy.start()
        for copy in copies:
            copy.wait()

    pl.run_scoped(run, pltpu.SemaphoreType.DMA((6,)))


def solution(mesh):
    in_specs = (
        P(None, "fsdp", "member"),
        P("fsdp", "member"),
        P("fsdp", "member"),
        P(None, "member"),
        P(None, "member"),
        P(None, "fsdp", "member"),
    )
    out_specs = (
        P(None, "fsdp", "member"),
        P(None, "fsdp", "member"),
        P("fsdp", "member"),
        P(None, "member"),
        P(None, "member"),
        P("fsdp", "member"),
    )
    members = mesh.shape["member"]
    chips = mesh.shape["fsdp"] // 2
    if members == 2 and chips >= 8 and chips & (chips - 1) == 0:
        per_device = functools.partial(fused, chips)
    else:
        per_device = general
    return jax.shard_map(
        per_device, mesh=mesh, in_specs=in_specs, out_specs=out_specs, check_vma=False
    )
```

```python
import functools

import jax
import jax.numpy as jnp
from jax import lax
from jax.experimental import pallas as pl
from jax.experimental.pallas import tpu as pltpu
from jax.sharding import PartitionSpec as P

F32 = jnp.float32
BF16 = jnp.bfloat16


def general(context, residual, out_weight, in_factor, out_factor, cotangent):
    in_wide = in_factor.astype(jnp.float32)
    out_wide = out_factor.astype(jnp.float32)
    scaled_local = (context.astype(jnp.float32) * in_wide[:, None, :]).astype(jnp.bfloat16)
    scaled_grad = (cotangent.astype(jnp.float32) * out_wide[:, None, :]).astype(jnp.bfloat16)
    scaled_context = lax.all_gather(scaled_local, "member", axis=2, tiled=True)
    weight = lax.all_gather(out_weight, "fsdp", axis=0, tiled=True)
    projected = jnp.einsum(
        "eti,id->etd", scaled_context, weight, preferred_element_type=jnp.float32
    )
    partial_value = jnp.einsum(
        "etd,id->eti", scaled_grad, weight, preferred_element_type=jnp.float32
    )
    hidden = (residual.astype(jnp.float32)[None] + projected * out_wide[:, None, :]).astype(
        jnp.bfloat16
    )
    backward = lax.psum_scatter(
        partial_value.astype(jnp.bfloat16), "member", scatter_dimension=2, tiled=True
    ).astype(jnp.float32)
    grad_context = (backward * in_wide[:, None, :]).astype(jnp.bfloat16)
    grad_in_local = jnp.sum(context.astype(jnp.float32) * backward, axis=1)
    grad_out_local = jnp.sum(cotangent.astype(jnp.float32) * projected, axis=1)
    grad_in, grad_out = lax.psum((grad_in_local, grad_out_local), "fsdp")
    grad_block = jnp.einsum(
        "eti,etd->id", scaled_context, scaled_grad, preferred_element_type=jnp.float32
    )
    grad_weight = lax.psum_scatter(grad_block, "fsdp", scatter_dimension=0, tiled=True)
    grad_residual = jnp.sum(cotangent.astype(jnp.float32), axis=0)
    return (hidden, grad_context, grad_weight, grad_in, grad_out, grad_residual)


def kernel(C, *refs):
    half = C // 2
    far = C // 2
    dma = pltpu.SemaphoreType.DMA
    pl.run_scoped(
        functools.partial(work, C, *refs),
        dma((6,)),
        dma((6,)),
        dma((12,)),
        dma((half + 1,)),
        dma((2 * far - 1,)),
        dma((far + 1,)),
        dma((half + 1,)),
        dma((C,)),
        dma((2 * far - 1,)),
        dma((6,)),
        pltpu.SemaphoreType.REGULAR,
    )


def work(
    C,
    ctx_h, res_h, w_h, inf_h, outf_h, cot_h,
    hid_o, gc_o, gw_o, gi_o, go_o, gr_o,
    hid, gc, gw, gi, go, gr,
    ctx, cot, res, inf, outf, cbuf, infx, sc, sg, wb, proj, part, xrecv, gall, psend, precv, rsend, rrecv,
    arb, ars, arr, fin, swp, swr,
    ld_sem, st_sem, out_sem, cx_rs, ag_rs, pt_rs, px_rs, ps_rs, rs_rs, ar_rs, ready,
):
    E, T, H = ctx.shape
    R = w_h.shape[0]
    R2 = 2 * R
    S = R // 2
    half = C // 2
    far = C // 2
    lines = C // 2
    H2 = H // 2
    pieces = 2 * far - 1

    m = lax.axis_index("member")
    f = lax.axis_index("fsdp")
    c = f % 2
    q = f // 2
    p = (1 - q % 2) * (q // 2) + (q % 2) * (C - 1 - q // 2)

    def chip_at(offset):
        pos = (p + offset + C) % C
        y = pos // half
        return 2 * ((1 - y) * pos + y * (C - 1 - pos)) + y

    peer = (1 - m, f)
    partner = (m, q * 2 + 1 - c)
    nxt = (m, chip_at(1) * 2 + c)
    prv = (m, chip_at(-1) * 2 + c)
    side = (nxt, prv)
    sign = (1, -1)
    beside = (m, f + 2 - 4 * (q % 2))

    def along(i):
        line = q // 2
        other = 0
        bit = 1
        while bit < lines:
            own = (line // bit) % 2
            other = other + bit * (1 - own if i & bit else own)
            bit *= 2
        return (m, f + 4 * (other - line))


    def rc(src, dst, ss, rs, dev):
        return pltpu.make_async_remote_copy(
            src_ref=src, dst_ref=dst, send_sem=ss, recv_sem=rs,
            device_id=dev, device_id_type=pl.DeviceIdType.MESH,
        )

    barrier = pltpu.get_barrier_semaphore()

    def greet(dev):
        pl.semaphore_signal(barrier, inc=1, device_id=dev, device_id_type=pl.DeviceIdType.MESH)

    lead, deputy = m * c == 1, m * (1 - c) == 1
    greet((1 - m, q * 2 + c + (1 - m) * (1 - c)))

    @pl.when(jnp.logical_not(lead))
    def _():
        greet(partner)

    for ahead in (1, -1):
        greet((m, chip_at(ahead) * 2 + c * (1 - m)))

    def rows_of(core):
        return pl.ds(pl.multiple_of(core * R, R), R)

    def load(i, src, dst):
        copy = pltpu.make_async_copy(src, dst, ld_sem.at[i])
        copy.start()
        return copy

    def store(i, src, dst):
        pltpu.make_async_copy(src, dst, st_sem.at[i]).start()

    CX, CXF, CXP, AG, PT, PX, PS, RS, AR, SWAP, SWP, FIN = range(12)

    ld_inf = load(0, inf_h, inf)
    ld_ctx = load(1, ctx_h, ctx)
    ld_outf = load(2, outf_h, outf)
    ld_cot = load(3, cot_h, cot)
    ld_w = load(4, w_h, wb.at[q, rows_of(c)])
    ld_res = load(5, res_h, res)

    order = [chip_at(-far)] + [chip_at(s * (far - k)) for k in range(1, far) for s in sign] + [q]

    def ranked(side_of):
        found = [0] * half
        count = 0
        for chip in order:
            member = chip // half == side_of
            for n in range(half):
                found[n] = jnp.where(jnp.logical_and(member, count == n), chip, found[n])
            count = count + jnp.where(member, 1, 0)
        return found

    mine = ranked(m)
    theirs = ranked(1 - m)

    def cols_of(chip):
        return pl.ds(pl.multiple_of((chip % half) * R2, R2), R2)

    def cx(n):
        return rc(ctx_h.at[:, :, cols_of(mine[n])], cbuf.at[n], out_sem.at[CX], cx_rs.at[n], peer)

    cxf = rc(inf_h, infx, out_sem.at[CXF], cx_rs.at[half], peer)

    cxp = rc(infx, infx, out_sem.at[CXP], cx_rs.at[half], partner)

    def pass_on():
        cxf.wait_recv()
        cxp.start()

    def sub(core, u):
        return pl.ds(pl.multiple_of(core * R + u * S, S), S)

    def ag(d, s, u, shift):
        qq = chip_at(-sign[d] * (s - 1 + shift))
        dst = wb.at[qq, sub(c, u)]
        src = w_h.at[pl.ds(u * S, S)] if (s == 1 and shift == 0) else dst
        return rc(src, dst, out_sem.at[AG], ag_rs.at[2 * (s - 1) + int(u != d)], side[d])

    def pt(s, u, offset, own):
        qq = chip_at(offset)
        dst = wb.at[qq, sub(c if own else 1 - c, u)]
        src = w_h.at[pl.ds(u * S, S)] if (own and s == 0) else dst
        return rc(src, dst, out_sem.at[PT], pt_rs.at[s], partner)

    def both_wait(sems, i):
        held = wb.at[q, rows_of(c)]
        rc(held, held, out_sem.at[AG], sems.at[i], nxt).wait_recv()

    def pt_wait(s):
        held = wb.at[q] if 0 < s < far else wb.at[q, rows_of(c)]
        rc(held, held, out_sem.at[PT], pt_rs.at[s], partner).wait_recv()

    def tell(sem):
        pl.semaphore_signal(sem, inc=1, device_id=partner, device_id_type=pl.DeviceIdType.MESH)

    @pl.when(jnp.logical_not(deputy))
    def _():
        pl.semaphore_wait(barrier, 4 - m)

    @pl.when(lead)
    def _():
        tell(ready)

    @pl.when(deputy)
    def _():
        pl.semaphore_wait(ready, 1)

    pl.when(c == 1)(cxf.start)
    for n in range(half):
        cx(n).start()

    @pl.when(deputy)
    def _():
        pl.semaphore_wait(barrier, 4)
        tell(ready)

    @pl.when(lead)
    def _():
        pl.semaphore_wait(ready, 1)

    for t in range(2):
        for d in range(2):
            ag(d, 1, d if t == 0 else 1 - d, 0).start()
        pt(0, t, 0, True).start()

    ld_inf.wait()
    ld_ctx.wait()
    inw = inf[...].astype(F32)
    for e in range(E):
        v = (ctx[e].astype(F32) * inw[e:e + 1]).astype(BF16)
        for j in range(half):
            sc[m * half + j, e * T:(e + 1) * T, :] = v[:, j * R2:(j + 1) * R2]
    ld_outf.wait()
    ld_cot.wait()
    outw = outf[...].astype(F32)
    for e in range(E):
        sg[e * T:(e + 1) * T, :] = (cot[e].astype(F32) * outw[e:e + 1]).astype(BF16)

    def px(qq, first, last=False):
        rows = pl.ds(0 if first else E * T // 2, E * T // 2)
        i = half if last else qq % half
        return rc(part.at[qq, rows], xrecv.at[qq % half, rows], out_sem.at[PX], px_rs.at[i], peer)

    def ps(qq):
        return rc(psend.at[qq], precv.at[qq], out_sem.at[PS], ps_rs.at[qq], partner)

    def gw_one(qq):
        g = lax.dot_general(sc[qq], sg[...], (((0,), (0,)), ((), ())), preferred_element_type=F32)
        gall[qq, 0] = g[:R]
        gall[qq, 1] = g[R:]
        psend[qq] = gall[qq, 1 - c].astype(BF16)
        ps(qq).start()

    def order_at(i):
        return chip_at((far - (i + 1) // 2) * (1 - 2 * ((i + 1) % 2)))

    def gw_mine():
        def body(i, carry):
            qq = order_at(i)

            @pl.when(qq // half == m)
            def _():
                gw_one(qq)
            return carry
        lax.fori_loop(0, C, body, 0)

    def project(qq):
        proj[...] += jnp.dot(sc[qq], wb[qq], preferred_element_type=F32)

    def process(offsets):
        def body(j, carry):
            off = offsets[0] if len(offsets) == 1 else offsets[0] + j * (offsets[1] - offsets[0])
            qq = chip_at(off)
            part[qq] = lax.dot_general(
                sg[...], wb[qq], (((1,), (1,)), ((), ())), preferred_element_type=F32
            ).astype(BF16)

            @pl.when(qq // half != m)
            def _():
                px(qq, True).start()

            @pl.when(jnp.logical_and(qq // half != m, qq != theirs[0]))
            def _():
                px(qq, False).start()

            @pl.when(qq // half == m)
            def _():
                project(qq)
            return carry
        lax.fori_loop(0, len(offsets), body, 0)

    def piece(k, u, d):
        return 2 * k - 1 + int(u == d) if k else 0

    def rs(d, k, u):
        i = piece(k, u, d)
        return rc(rsend.at[d, i], rrecv.at[d, i], out_sem.at[RS], rs_rs.at[i], side[d])

    def chip_sum(qq, u):
        rows = slice(u * S, (u + 1) * S)
        return gall[qq, c, rows, :] + precv[qq, rows, :].astype(F32)

    def rs_sub(k, late):
        chips = [chip_at(sign[d] * (far - k)) if k else chip_at(-far) for d in range(2)]
        if k == 0:
            ps(chips[0]).wait_recv()
        elif not late:
            for d in range(2):
                ps(chips[d]).wait_recv()
        held = k > 1 or (k == 1 and late)
        if held:
            both_wait(rs_rs, piece(k - 1, int(late), 1))
        for d in range(2):
            u = d if late else 1 - d
            v = chip_sum(chips[d], u)
            if held:
                v = v + rrecv[d, piece(k - 1, u, d)].astype(F32)
            rsend[d, piece(k, u, d)] = v.astype(BF16)
            rs(d, k, u).start()

    proj[...] = jnp.zeros(proj.shape, F32)
    gw_mine()
    ld_w.wait()
    pt_wait(0)
    process([0])

    def scale_in(n):
        cx(n).wait_recv()
        for e in range(E):
            wide = infx[e:e + 1, cols_of(theirs[n])].astype(F32)
            sc[theirs[n], e * T:(e + 1) * T, :] = (cbuf[n, e].astype(F32) * wide).astype(BF16)
        gw_one(theirs[n])

    def forward(s, t):
        both_wait(ag_rs, 2 * (s - 1) + t)
        for d in range(2):
            u = d if t == 0 else 1 - d
            if s + 1 < far or (s + 1 == far and t == 0):
                ag(d, s + 1, u, 0).start()
            pt(s, u, -sign[d] * s, True).start()

    for s in range(1, far):
        forward(s, 0)
        if s == far - 1:
            rs_sub(0, True)
        if s == 1:
            gr[...] = jnp.sum(cot[...].astype(F32), axis=0)
            store(1, gr, gr_o)
        else:
            pt_wait(s - 1)
            process([1 - s])
        forward(s, 1)
        if s == 1:
            pl.when(c == 1)(pass_on)
        if s > 1:
            process([s - 1])
            if s == 2:
                pl.when(c == 0)(cxp.wait_recv)
            scale_in(s - 2)
    scale_in(far - 2)
    both_wait(ag_rs, 2 * (far - 1))
    for d in range(2):
        pt(far, d, far, True).start()
    pt_wait(far - 1)
    process([1 - far])
    rs_sub(1, False)
    process([far - 1])
    pt_wait(far)
    process([far])
    for n in range(far - 1):
        project(theirs[n])
    rs_sub(1, True)
    for n in range(far - 1, half):
        scale_in(n)
        project(theirs[n])

    ld_res.wait()
    resw = res[...].astype(F32)
    for e in range(E):
        pe = proj[e * T:(e + 1) * T, :]
        hid[e] = (resw + pe * outw[e:e + 1]).astype(BF16)
        a = jnp.sum(cot[e].astype(F32) * pe, axis=0, keepdims=True)
        for h in range(2):
            arb[h, 2 * E + e:2 * E + e + 1, :] = a[:, h * H2:(h + 1) * H2]
    store(0, hid, hid_o)
    for n in range(half):
        h, first = n * R2 // H2, n * R2 % H2
        slot = theirs[n] % half
        ahead = slot * R2 // H2
        far_cols = pl.ds(pl.multiple_of(slot * R2 - ahead * H2, R2), R2)
        for e in range(E):
            rows = slice(e * T, (e + 1) * T)
            a = ctx[e, :, n * R2:(n + 1) * R2].astype(F32) * part[m * half + n, rows, :].astype(F32)
            arb[h, e:e + 1, first:first + R2] = jnp.sum(a, axis=0, keepdims=True)
            a = cbuf[n, e].astype(F32) * part[theirs[n], rows, :].astype(F32)
            arb[ahead, E + e:E + e + 1, far_cols] = jnp.sum(a, axis=0, keepdims=True)

    def ar(i, src, dev):
        return rc(src, arr.at[i], out_sem.at[AR], ar_rs.at[min(i, 2)], dev)

    to_partner = ar(0, arb.at[1 - c], partner)
    to_beside = ar(1, ars.at[0], beside)
    to_lines = [ar(1 + i, ars.at[1], along(i)) for i in range(1, lines)]
    from_lines = rc(arr.at[2:], arr.at[2:], out_sem.at[AR], ar_rs.at[2], partner)
    to_other = rc(fin.at[0], fin.at[1], out_sem.at[FIN], ar_rs.at[3], partner)
    swap = rc(swp, swr.at[c], out_sem.at[SWAP], ar_rs.at[4], peer)
    swap_on = rc(swr.at[c], swr.at[c], out_sem.at[SWP], ar_rs.at[5], partner)

    own_half = pl.ds(pl.multiple_of(c * H2, H2), H2)
    other_half = pl.ds(pl.multiple_of((1 - c) * H2, H2), H2)

    def ar_step(i):
        if i == 0:
            to_partner.wait_recv()
            ars[0] = arb[c] + arr[0]
            to_beside.start()
        elif i == 1:
            to_beside.wait_recv()
            ars[1] = ars[0] + arr[1]
            for copy in to_lines:
                copy.start()
        else:
            from_lines.wait_recv()
            total = ars[1]
            for n in range(2, lines + 1):
                total = total + arr[n]
            swp[...] = total[E:2 * E]
            fin[0, :E] = total[:E]
            fin[0, E:] = total[2 * E:]
            swap.start()
            to_other.start()

    def finish(n, members, i):
        chip = mine[n]
        slot = chip % half
        held = xrecv.at[slot, pl.ds(members[0] * T, len(members) * T)]
        rc(held, held, out_sem.at[PX], px_rs.at[i], peer).wait_recv()
        for e in members:
            rows = slice(e * T, (e + 1) * T)
            be = part[chip, rows, :].astype(F32) + xrecv[slot, rows, :].astype(F32)
            wide = inf[e:e + 1, cols_of(chip)].astype(F32)
            gc[e, :, cols_of(chip)] = (be * wide).astype(BF16)
        rows = pl.ds(members[0], len(members))
        store(2, gc.at[rows, :, cols_of(chip)], gc_o.at[rows, :, cols_of(chip)])

    every = range(E)

    to_partner.start()
    pending = half
    for k in range(2, far):
        rs_sub(k, False)
        if k == 2:
            ar_step(0)
        rs_sub(k, True)
        if k == 2:
            ar_step(1)
        if pending > 2:
            pending -= 1
            finish(pending, every, mine[pending] % half)
    ar_step(2)
    px(theirs[0], False, True).start()
    ps(q).wait_recv()
    for t in range(2):
        both_wait(rs_rs, piece(far - 1, t, 1))
    for u in range(2):
        rows = slice(u * S, (u + 1) * S)
        total = chip_sum(q, u)
        for d in range(2):
            total = total + rrecv[d, piece(far - 1, u, d)].astype(F32)
        gw[rows, :] = total
        store(3, gw.at[pl.ds(u * S, S)], gw_o.at[pl.ds(u * S, S)])
    to_other.wait_recv()
    go[:, own_half] = fin[0, E:]
    go[:, other_half] = fin[1, E:]
    store(4, go, go_o)
    while pending > 1:
        pending -= 1
        finish(pending, every, mine[pending] % half)
    swap.wait_recv()
    swap_on.start()
    finish(0, every[:E // 2], mine[0] % half)
    finish(0, every[E // 2:], half)
    swap_on.wait_recv()
    gi[:, own_half] = fin[0, :E] + swr[c]
    gi[:, other_half] = fin[1, :E] + swr[1 - c]
    store(5, gi, gi_o)

    sent = (
        (CX, cbuf), (AG, rsend), (PT, psend), (PX, xrecv),
        (PS, psend), (RS, rsend), (AR, arr), (SWAP, swp), (SWP, swp), (FIN, fin.at[0]),
    )
    for i, ref in sent:
        rc(ref, ref, out_sem.at[i], ar_rs.at[4], peer).wait_send()

    @pl.when(c == 1)
    def _():
        cxf.wait_send()
        cxp.wait_send()

    stored = ((hid, hid_o), (gr, gr_o), (gc, gc_o), (gw, gw_o), (go, go_o), (gi, gi_o))
    for i, (src, dst) in enumerate(stored):
        pltpu.make_async_copy(src, dst, st_sem.at[i]).wait()


def fused(C, context, residual, out_weight, in_factor, out_factor, cotangent):
    E, T, H = context.shape
    M = E * T
    R = out_weight.shape[0]
    half = C // 2
    far = half
    lines = C // 2
    pieces = 2 * far - 1
    hbm = pl.BlockSpec(memory_space=pl.ANY)
    shape = jax.ShapeDtypeStruct
    results = pl.pallas_call(
        functools.partial(kernel, C),
        out_shape=(
            pltpu.VMEM((E, T, H), BF16),
            pltpu.VMEM((E, T, H), BF16),
            pltpu.VMEM((R, H), F32),
            pltpu.VMEM((E, H), F32),
            pltpu.VMEM((E, H), F32),
            pltpu.VMEM((T, H), F32),
        ),
        in_specs=[hbm] * 6,
        out_specs=tuple([hbm] * 6),
        scratch_shapes=[
            pltpu.VMEM((E, T, H), BF16),
            pltpu.VMEM((E, T, H), BF16),
            pltpu.VMEM((R, H), F32),
            pltpu.VMEM((E, H), F32),
            pltpu.VMEM((E, H), F32),
            pltpu.VMEM((T, H), F32),
            pltpu.VMEM((E, T, H), BF16),
            pltpu.VMEM((E, T, H), BF16),
            pltpu.VMEM((T, H), BF16),
            pltpu.VMEM((E, H), BF16),
            pltpu.VMEM((E, H), BF16),
            pltpu.VMEM((half, E, T, 2 * R), BF16),
            pltpu.VMEM((E, H), BF16),
            pltpu.VMEM((C, M, 2 * R), BF16),
            pltpu.VMEM((M, H), BF16),
            pltpu.VMEM((C, 2 * R, H), BF16),
            pltpu.VMEM((M, H), F32),
            pltpu.VMEM((C, M, 2 * R), BF16),
            pltpu.VMEM((half, M, 2 * R), BF16),
            pltpu.VMEM((C, 2, R, H), F32),
            pltpu.VMEM((C, R, H), BF16),
            pltpu.VMEM((C, R, H), BF16),
            pltpu.VMEM((2, pieces, R // 2, H), BF16),
            pltpu.VMEM((2, pieces, R // 2, H), BF16),
            pltpu.VMEM((2, 3 * E, H // 2), F32),
            pltpu.VMEM((2, 3 * E, H // 2), F32),
            pltpu.VMEM((lines + 1, 3 * E, H // 2), F32),
            pltpu.VMEM((2, 2 * E, H // 2), F32),
            pltpu.VMEM((E, H // 2), F32),
            pltpu.VMEM((2, E, H // 2), F32),
        ],
        compiler_params=pltpu.CompilerParams(
            collective_id=0, has_side_effects=True, vmem_limit_bytes=62208 * 1024
        ),
    )(context, residual, out_weight, in_factor, out_factor, cotangent)
    return pl.pallas_call(
        deliver,
        out_shape=tuple(shape(r.shape, r.dtype) for r in results),
        in_specs=[hbm] * 6,
        out_specs=tuple([hbm] * 6),
        compiler_params=pltpu.CompilerParams(vmem_limit_bytes=1024 * 1024),
    )(*results)


def deliver(*refs):
    def run(sem):
        copies = [pltpu.make_async_copy(refs[i], refs[6 + i], sem.at[i]) for i in range(6)]
        for copy in copies:
            copy.start()
        for copy in copies:
            copy.wait()

    pl.run_scoped(run, pltpu.SemaphoreType.DMA((6,)))


def solution(mesh):
    in_specs = (
        P(None, "fsdp", "member"),
        P("fsdp", "member"),
        P("fsdp", "member"),
        P(None, "member"),
        P(None, "member"),
        P(None, "fsdp", "member"),
    )
    out_specs = (
        P(None, "fsdp", "member"),
        P(None, "fsdp", "member"),
        P("fsdp", "member"),
        P(None, "member"),
        P(None, "member"),
        P("fsdp", "member"),
    )
    members = mesh.shape["member"]
    chips = mesh.shape["fsdp"] // 2
    if members == 2 and chips >= 8 and chips & (chips - 1) == 0:
        per_device = functools.partial(fused, chips)
    else:
        per_device = general
    return jax.shard_map(
        per_device, mesh=mesh, in_specs=in_specs, out_specs=out_specs, check_vma=False
    )
```

```python
import functools

import jax
import jax.numpy as jnp
from jax import lax
from jax.experimental import pallas as pl
from jax.experimental.pallas import tpu as pltpu
from jax.sharding import PartitionSpec as P

F32 = jnp.float32
BF16 = jnp.bfloat16


def general(context, residual, out_weight, in_factor, out_factor, cotangent):
    in_wide = in_factor.astype(jnp.float32)
    out_wide = out_factor.astype(jnp.float32)
    scaled_local = (context.astype(jnp.float32) * in_wide[:, None, :]).astype(jnp.bfloat16)
    scaled_grad = (cotangent.astype(jnp.float32) * out_wide[:, None, :]).astype(jnp.bfloat16)
    scaled_context = lax.all_gather(scaled_local, "member", axis=2, tiled=True)
    weight = lax.all_gather(out_weight, "fsdp", axis=0, tiled=True)
    projected = jnp.einsum(
        "eti,id->etd", scaled_context, weight, preferred_element_type=jnp.float32
    )
    partial_value = jnp.einsum(
        "etd,id->eti", scaled_grad, weight, preferred_element_type=jnp.float32
    )
    hidden = (residual.astype(jnp.float32)[None] + projected * out_wide[:, None, :]).astype(
        jnp.bfloat16
    )
    backward = lax.psum_scatter(
        partial_value.astype(jnp.bfloat16), "member", scatter_dimension=2, tiled=True
    ).astype(jnp.float32)
    grad_context = (backward * in_wide[:, None, :]).astype(jnp.bfloat16)
    grad_in_local = jnp.sum(context.astype(jnp.float32) * backward, axis=1)
    grad_out_local = jnp.sum(cotangent.astype(jnp.float32) * projected, axis=1)
    grad_in, grad_out = lax.psum((grad_in_local, grad_out_local), "fsdp")
    grad_block = jnp.einsum(
        "eti,etd->id", scaled_context, scaled_grad, preferred_element_type=jnp.float32
    )
    grad_weight = lax.psum_scatter(grad_block, "fsdp", scatter_dimension=0, tiled=True)
    grad_residual = jnp.sum(cotangent.astype(jnp.float32), axis=0)
    return (hidden, grad_context, grad_weight, grad_in, grad_out, grad_residual)


def kernel(C, *refs):
    half = C // 2
    far = C // 2
    dma = pltpu.SemaphoreType.DMA
    pl.run_scoped(
        functools.partial(work, C, *refs),
        dma((6,)),
        dma((6,)),
        dma((13,)),
        dma((half + 1,)),
        dma((2 * far - 1,)),
        dma((far + 1,)),
        dma((half + 1,)),
        dma((C,)),
        dma((2 * far - 1,)),
        dma((7,)),
        pltpu.SemaphoreType.REGULAR,
    )


def work(
    C,
    ctx_h, res_h, w_h, inf_h, outf_h, cot_h,
    hid_o, gc_o, gw_o, gi_o, go_o, gr_o,
    hid, gc, gw, gi, go, gr,
    ctx, cot, res, inf, outf, cbuf, infx, sc, sg, wb, proj, part, xrecv, gall, psend, precv, rsend, rrecv,
    arb, ars, arr, fin, swp, swr, relay,
    ld_sem, st_sem, out_sem, cx_rs, ag_rs, pt_rs, px_rs, ps_rs, rs_rs, ar_rs, ready,
):
    E, T, H = ctx.shape
    R = w_h.shape[0]
    R2 = 2 * R
    S = R // 2
    half = C // 2
    far = C // 2
    lines = C // 2
    H2 = H // 2
    pieces = 2 * far - 1

    m = lax.axis_index("member")
    f = lax.axis_index("fsdp")
    c = f % 2
    q = f // 2
    p = (1 - q % 2) * (q // 2) + (q % 2) * (C - 1 - q // 2)

    def chip_at(offset):
        pos = (p + offset + C) % C
        y = pos // half
        return 2 * ((1 - y) * pos + y * (C - 1 - pos)) + y

    peer = (1 - m, f)
    partner = (m, q * 2 + 1 - c)
    nxt = (m, chip_at(1) * 2 + c)
    prv = (m, chip_at(-1) * 2 + c)
    side = (nxt, prv)
    sign = (1, -1)
    beside = (m, f + 2 - 4 * (q % 2))

    def along(i):
        line = q // 2
        other = 0
        bit = 1
        while bit < lines:
            own = (line // bit) % 2
            other = other + bit * (1 - own if i & bit else own)
            bit *= 2
        return (m, f + 4 * (other - line))


    def rc(src, dst, ss, rs, dev):
        return pltpu.make_async_remote_copy(
            src_ref=src, dst_ref=dst, send_sem=ss, recv_sem=rs,
            device_id=dev, device_id_type=pl.DeviceIdType.MESH,
        )

    barrier = pltpu.get_barrier_semaphore()

    def greet(dev):
        pl.semaphore_signal(barrier, inc=1, device_id=dev, device_id_type=pl.DeviceIdType.MESH)

    lead, deputy = m * c == 1, m * (1 - c) == 1
    greet((1 - m, q * 2 + c + (1 - m) * (1 - c)))

    @pl.when(jnp.logical_not(lead))
    def _():
        greet(partner)

    for ahead in (1, -1):
        greet((m, chip_at(ahead) * 2 + c * (1 - m)))

    def rows_of(core):
        return pl.ds(pl.multiple_of(core * R, R), R)

    def load(i, src, dst):
        copy = pltpu.make_async_copy(src, dst, ld_sem.at[i])
        copy.start()
        return copy

    def store(i, src, dst):
        pltpu.make_async_copy(src, dst, st_sem.at[i]).start()

    CX, CXF, CXP, AG, PT, PX, PS, RS, AR, SWAP, SWP, FIN, RELAY = range(13)

    ld_inf = load(0, inf_h, inf)
    ld_ctx = load(1, ctx_h, ctx)
    ld_outf = load(2, outf_h, outf)
    ld_cot = load(3, cot_h, cot)
    ld_w = load(4, w_h, wb.at[q, rows_of(c)])
    ld_res = load(5, res_h, res)

    order = [chip_at(-far)] + [chip_at(s * (far - k)) for k in range(1, far) for s in sign] + [q]

    def ranked(side_of):
        found = [0] * half
        count = 0
        for chip in order:
            member = chip // half == side_of
            for n in range(half):
                found[n] = jnp.where(jnp.logical_and(member, count == n), chip, found[n])
            count = count + jnp.where(member, 1, 0)
        return found

    mine = ranked(m)
    theirs = ranked(1 - m)

    def cols_of(chip):
        return pl.ds(pl.multiple_of((chip % half) * R2, R2), R2)

    def cx(n):
        return rc(ctx_h.at[:, :, cols_of(mine[n])], cbuf.at[n], out_sem.at[CX], cx_rs.at[n], peer)

    cxf = rc(inf_h, infx, out_sem.at[CXF], cx_rs.at[half], peer)

    cxp = rc(infx, infx, out_sem.at[CXP], cx_rs.at[half], partner)

    def pass_on():
        cxf.wait_recv()
        cxp.start()

    def sub(core, u):
        return pl.ds(pl.multiple_of(core * R + u * S, S), S)

    def ag(d, s, u, shift):
        qq = chip_at(-sign[d] * (s - 1 + shift))
        dst = wb.at[qq, sub(c, u)]
        src = w_h.at[pl.ds(u * S, S)] if (s == 1 and shift == 0) else dst
        return rc(src, dst, out_sem.at[AG], ag_rs.at[2 * (s - 1) + int(u != d)], side[d])

    def pt(s, u, offset, own):
        qq = chip_at(offset)
        dst = wb.at[qq, sub(c if own else 1 - c, u)]
        src = w_h.at[pl.ds(u * S, S)] if (own and s == 0) else dst
        return rc(src, dst, out_sem.at[PT], pt_rs.at[s], partner)

    def both_wait(sems, i):
        held = wb.at[q, rows_of(c)]
        rc(held, held, out_sem.at[AG], sems.at[i], nxt).wait_recv()

    def pt_wait(s):
        held = wb.at[q] if 0 < s < far else wb.at[q, rows_of(c)]
        rc(held, held, out_sem.at[PT], pt_rs.at[s], partner).wait_recv()

    def tell(sem):
        pl.semaphore_signal(sem, inc=1, device_id=partner, device_id_type=pl.DeviceIdType.MESH)

    @pl.when(jnp.logical_not(deputy))
    def _():
        pl.semaphore_wait(barrier, 4 - m)

    @pl.when(lead)
    def _():
        tell(ready)

    @pl.when(deputy)
    def _():
        pl.semaphore_wait(ready, 1)

    pl.when(c == 1)(cxf.start)
    for n in range(half):
        cx(n).start()

    @pl.when(deputy)
    def _():
        pl.semaphore_wait(barrier, 4)
        tell(ready)

    @pl.when(lead)
    def _():
        pl.semaphore_wait(ready, 1)

    for t in range(2):
        for d in range(2):
            ag(d, 1, d if t == 0 else 1 - d, 0).start()
        pt(0, t, 0, True).start()

    ld_inf.wait()
    ld_ctx.wait()
    inw = inf[...].astype(F32)
    for e in range(E):
        v = (ctx[e].astype(F32) * inw[e:e + 1]).astype(BF16)
        for j in range(half):
            sc[m * half + j, e * T:(e + 1) * T, :] = v[:, j * R2:(j + 1) * R2]
    ld_outf.wait()
    ld_cot.wait()
    outw = outf[...].astype(F32)
    for e in range(E):
        sg[e * T:(e + 1) * T, :] = (cot[e].astype(F32) * outw[e:e + 1]).astype(BF16)

    def px(qq, first, end, last=False):
        rows = pl.ds(first * T, (end - first) * T)
        i = half if last else qq % half
        return rc(part.at[qq, rows], xrecv.at[qq % half, rows], out_sem.at[PX], px_rs.at[i], peer)

    last_rows = pl.ds((E - 1) * T, T)
    relay_in = rc(part.at[theirs[0], last_rows], relay, out_sem.at[PX], ar_rs.at[6], partner)
    relay_out = rc(
        relay, xrecv.at[theirs[0] % half, last_rows], out_sem.at[RELAY], px_rs.at[half], (1 - m, q * 2)
    )

    def ps(qq):
        return rc(psend.at[qq], precv.at[qq], out_sem.at[PS], ps_rs.at[qq], partner)

    def gw_one(qq):
        g = lax.dot_general(sc[qq], sg[...], (((0,), (0,)), ((), ())), preferred_element_type=F32)
        gall[qq, 0] = g[:R]
        gall[qq, 1] = g[R:]
        psend[qq] = gall[qq, 1 - c].astype(BF16)
        ps(qq).start()

    def order_at(i):
        return chip_at((far - (i + 1) // 2) * (1 - 2 * ((i + 1) % 2)))

    def gw_mine():
        def body(i, carry):
            qq = order_at(i)

            @pl.when(qq // half == m)
            def _():
                gw_one(qq)
            return carry
        lax.fori_loop(0, C, body, 0)

    def project(qq):
        proj[...] += jnp.dot(sc[qq], wb[qq], preferred_element_type=F32)

    def process(offsets):
        def body(j, carry):
            off = offsets[0] if len(offsets) == 1 else offsets[0] + j * (offsets[1] - offsets[0])
            qq = chip_at(off)
            part[qq] = lax.dot_general(
                sg[...], wb[qq], (((1,), (1,)), ((), ())), preferred_element_type=F32
            ).astype(BF16)

            @pl.when(jnp.logical_and(qq // half != m, qq != theirs[0]))
            def _():
                px(qq, 0, E).start()

            @pl.when(jnp.logical_and(c == 1, qq == theirs[0]))
            def _():
                px(qq, 0, E - 1).start()

            @pl.when(jnp.logical_and(c == 0, qq == theirs[0]))
            def _():
                px(qq, 0, E - 2).start()
                relay_in.start()

            @pl.when(qq // half == m)
            def _():
                project(qq)
            return carry
        lax.fori_loop(0, len(offsets), body, 0)

    def piece(k, u, d):
        return 2 * k - 1 + int(u == d) if k else 0

    def rs(d, k, u):
        i = piece(k, u, d)
        return rc(rsend.at[d, i], rrecv.at[d, i], out_sem.at[RS], rs_rs.at[i], side[d])

    def chip_sum(qq, u):
        rows = slice(u * S, (u + 1) * S)
        return gall[qq, c, rows, :] + precv[qq, rows, :].astype(F32)

    def rs_sub(k, late):
        chips = [chip_at(sign[d] * (far - k)) if k else chip_at(-far) for d in range(2)]
        if k == 0:
            ps(chips[0]).wait_recv()
        elif not late:
            for d in range(2):
                ps(chips[d]).wait_recv()
        held = k > 1 or (k == 1 and late)
        if held:
            both_wait(rs_rs, piece(k - 1, int(late), 1))
        for d in range(2):
            u = d if late else 1 - d
            v = chip_sum(chips[d], u)
            if held:
                v = v + rrecv[d, piece(k - 1, u, d)].astype(F32)
            rsend[d, piece(k, u, d)] = v.astype(BF16)
            rs(d, k, u).start()

    proj[...] = jnp.zeros(proj.shape, F32)
    gw_mine()
    ld_w.wait()
    pt_wait(0)
    process([0])

    def scale_in(n):
        cx(n).wait_recv()
        for e in range(E):
            wide = infx[e:e + 1, cols_of(theirs[n])].astype(F32)
            sc[theirs[n], e * T:(e + 1) * T, :] = (cbuf[n, e].astype(F32) * wide).astype(BF16)
        gw_one(theirs[n])

    def forward(s, t):
        both_wait(ag_rs, 2 * (s - 1) + t)
        for d in range(2):
            u = d if t == 0 else 1 - d
            if s + 1 < far or (s + 1 == far and t == 0):
                ag(d, s + 1, u, 0).start()
            pt(s, u, -sign[d] * s, True).start()

    for s in range(1, far):
        forward(s, 0)
        if s == far - 1:
            rs_sub(0, True)
        if s == 1:
            gr[...] = jnp.sum(cot[...].astype(F32), axis=0)
            store(1, gr, gr_o)
        else:
            pt_wait(s - 1)
            process([1 - s])
        forward(s, 1)
        if s == 1:
            pl.when(c == 1)(pass_on)
        if s > 1:
            process([s - 1])
            if s == 2:
                pl.when(c == 0)(cxp.wait_recv)
            scale_in(s - 2)
    scale_in(far - 2)
    both_wait(ag_rs, 2 * (far - 1))
    for d in range(2):
        pt(far, d, far, True).start()
    pt_wait(far - 1)
    process([1 - far])
    rs_sub(1, False)
    process([far - 1])
    pt_wait(far)
    process([far])
    for n in range(far - 1):
        project(theirs[n])
    rs_sub(1, True)
    for n in range(far - 1, half):
        scale_in(n)
        project(theirs[n])

    ld_res.wait()
    resw = res[...].astype(F32)
    for e in range(E):
        pe = proj[e * T:(e + 1) * T, :]
        hid[e] = (resw + pe * outw[e:e + 1]).astype(BF16)
        a = jnp.sum(cot[e].astype(F32) * pe, axis=0, keepdims=True)
        for h in range(2):
            arb[h, 2 * E + e:2 * E + e + 1, :] = a[:, h * H2:(h + 1) * H2]
    store(0, hid, hid_o)
    for n in range(half):
        h, first = n * R2 // H2, n * R2 % H2
        slot = theirs[n] % half
        ahead = slot * R2 // H2
        far_cols = pl.ds(pl.multiple_of(slot * R2 - ahead * H2, R2), R2)
        for e in range(E):
            rows = slice(e * T, (e + 1) * T)
            a = ctx[e, :, n * R2:(n + 1) * R2].astype(F32) * part[m * half + n, rows, :].astype(F32)
            arb[h, e:e + 1, first:first + R2] = jnp.sum(a, axis=0, keepdims=True)
            a = cbuf[n, e].astype(F32) * part[theirs[n], rows, :].astype(F32)
            arb[ahead, E + e:E + e + 1, far_cols] = jnp.sum(a, axis=0, keepdims=True)

    def ar(i, src, dev):
        return rc(src, arr.at[i], out_sem.at[AR], ar_rs.at[min(i, 2)], dev)

    to_partner = ar(0, arb.at[1 - c], partner)
    to_beside = ar(1, ars.at[0], beside)
    to_lines = [ar(1 + i, ars.at[1], along(i)) for i in range(1, lines)]
    from_lines = rc(arr.at[2:], arr.at[2:], out_sem.at[AR], ar_rs.at[2], partner)
    to_other = rc(fin.at[0], fin.at[1], out_sem.at[FIN], ar_rs.at[3], partner)
    swap = rc(swp, swr.at[c], out_sem.at[SWAP], ar_rs.at[4], peer)
    swap_on = rc(swr.at[c], swr.at[c], out_sem.at[SWP], ar_rs.at[5], partner)

    own_half = pl.ds(pl.multiple_of(c * H2, H2), H2)
    other_half = pl.ds(pl.multiple_of((1 - c) * H2, H2), H2)

    def ar_step(i):
        if i == 0:
            to_partner.wait_recv()
            ars[0] = arb[c] + arr[0]
            to_beside.start()
        elif i == 1:
            to_beside.wait_recv()
            ars[1] = ars[0] + arr[1]
            for copy in to_lines:
                copy.start()
        else:
            from_lines.wait_recv()
            total = ars[1]
            for n in range(2, lines + 1):
                total = total + arr[n]
            swp[...] = total[E:2 * E]
            fin[0, :E] = total[:E]
            fin[0, E:] = total[2 * E:]
            swap.start()
            to_other.start()

    def finish(n, members, i):
        chip = mine[n]
        slot = chip % half
        held = xrecv.at[slot, pl.ds(members[0] * T, len(members) * T)]
        rc(held, held, out_sem.at[PX], px_rs.at[i], peer).wait_recv()
        for e in members:
            rows = slice(e * T, (e + 1) * T)
            be = part[chip, rows, :].astype(F32) + xrecv[slot, rows, :].astype(F32)
            wide = inf[e:e + 1, cols_of(chip)].astype(F32)
            gc[e, :, cols_of(chip)] = (be * wide).astype(BF16)
        rows = pl.ds(members[0], len(members))
        store(2, gc.at[rows, :, cols_of(chip)], gc_o.at[rows, :, cols_of(chip)])

    every = range(E)

    to_partner.start()
    pending = half
    for k in range(2, far):
        rs_sub(k, False)
        if k == 2:
            ar_step(0)
        rs_sub(k, True)
        if k == 2:
            ar_step(1)
        if pending > 2:
            pending -= 1
            finish(pending, every, mine[pending] % half)
    ar_step(2)

    @pl.when(c == 1)
    def _():
        relay_in.wait_recv()
        relay_out.start()
        px(theirs[0], E - 1, E, True).start()

    @pl.when(c == 0)
    def _():
        px(theirs[0], E - 2, E - 1).start()

    ps(q).wait_recv()
    for t in range(2):
        both_wait(rs_rs, piece(far - 1, t, 1))
    for u in range(2):
        rows = slice(u * S, (u + 1) * S)
        total = chip_sum(q, u)
        for d in range(2):
            total = total + rrecv[d, piece(far - 1, u, d)].astype(F32)
        gw[rows, :] = total
        store(3, gw.at[pl.ds(u * S, S)], gw_o.at[pl.ds(u * S, S)])
    to_other.wait_recv()
    go[:, own_half] = fin[0, E:]
    go[:, other_half] = fin[1, E:]
    store(4, go, go_o)
    while pending > 1:
        pending -= 1
        finish(pending, every, mine[pending] % half)
    swap.wait_recv()
    swap_on.start()
    finish(0, every[:E - 1], mine[0] % half)
    finish(0, every[E - 1:], half)
    swap_on.wait_recv()
    gi[:, own_half] = fin[0, :E] + swr[c]
    gi[:, other_half] = fin[1, :E] + swr[1 - c]
    store(5, gi, gi_o)

    sent = (
        (CX, cbuf), (AG, rsend), (PT, psend), (PX, xrecv),
        (PS, psend), (RS, rsend), (AR, arr), (SWAP, swp), (SWP, swp), (FIN, fin.at[0]),
    )
    for i, ref in sent:
        rc(ref, ref, out_sem.at[i], ar_rs.at[4], peer).wait_send()

    @pl.when(c == 1)
    def _():
        cxf.wait_send()
        cxp.wait_send()
        relay_out.wait_send()

    stored = ((hid, hid_o), (gr, gr_o), (gc, gc_o), (gw, gw_o), (go, go_o), (gi, gi_o))
    for i, (src, dst) in enumerate(stored):
        pltpu.make_async_copy(src, dst, st_sem.at[i]).wait()


def fused(C, context, residual, out_weight, in_factor, out_factor, cotangent):
    E, T, H = context.shape
    M = E * T
    R = out_weight.shape[0]
    half = C // 2
    far = half
    lines = C // 2
    pieces = 2 * far - 1
    hbm = pl.BlockSpec(memory_space=pl.ANY)
    shape = jax.ShapeDtypeStruct
    results = pl.pallas_call(
        functools.partial(kernel, C),
        out_shape=(
            pltpu.VMEM((E, T, H), BF16),
            pltpu.VMEM((E, T, H), BF16),
            pltpu.VMEM((R, H), F32),
            pltpu.VMEM((E, H), F32),
            pltpu.VMEM((E, H), F32),
            pltpu.VMEM((T, H), F32),
        ),
        in_specs=[hbm] * 6,
        out_specs=tuple([hbm] * 6),
        scratch_shapes=[
            pltpu.VMEM((E, T, H), BF16),
            pltpu.VMEM((E, T, H), BF16),
            pltpu.VMEM((R, H), F32),
            pltpu.VMEM((E, H), F32),
            pltpu.VMEM((E, H), F32),
            pltpu.VMEM((T, H), F32),
            pltpu.VMEM((E, T, H), BF16),
            pltpu.VMEM((E, T, H), BF16),
            pltpu.VMEM((T, H), BF16),
            pltpu.VMEM((E, H), BF16),
            pltpu.VMEM((E, H), BF16),
            pltpu.VMEM((half, E, T, 2 * R), BF16),
            pltpu.VMEM((E, H), BF16),
            pltpu.VMEM((C, M, 2 * R), BF16),
            pltpu.VMEM((M, H), BF16),
            pltpu.VMEM((C, 2 * R, H), BF16),
            pltpu.VMEM((M, H), F32),
            pltpu.VMEM((C, M, 2 * R), BF16),
            pltpu.VMEM((half, M, 2 * R), BF16),
            pltpu.VMEM((C, 2, R, H), F32),
            pltpu.VMEM((C, R, H), BF16),
            pltpu.VMEM((C, R, H), BF16),
            pltpu.VMEM((2, pieces, R // 2, H), BF16),
            pltpu.VMEM((2, pieces, R // 2, H), BF16),
            pltpu.VMEM((2, 3 * E, H // 2), F32),
            pltpu.VMEM((2, 3 * E, H // 2), F32),
            pltpu.VMEM((lines + 1, 3 * E, H // 2), F32),
            pltpu.VMEM((2, 2 * E, H // 2), F32),
            pltpu.VMEM((E, H // 2), F32),
            pltpu.VMEM((2, E, H // 2), F32),
            pltpu.VMEM((T, 2 * R), BF16),
        ],
        compiler_params=pltpu.CompilerParams(
            collective_id=0, has_side_effects=True, vmem_limit_bytes=62208 * 1024
        ),
    )(context, residual, out_weight, in_factor, out_factor, cotangent)
    return pl.pallas_call(
        deliver,
        out_shape=tuple(shape(r.shape, r.dtype) for r in results),
        in_specs=[hbm] * 6,
        out_specs=tuple([hbm] * 6),
        compiler_params=pltpu.CompilerParams(vmem_limit_bytes=1024 * 1024),
    )(*results)


def deliver(*refs):
    def run(sem):
        copies = [pltpu.make_async_copy(refs[i], refs[6 + i], sem.at[i]) for i in range(6)]
        for copy in copies:
            copy.start()
        for copy in copies:
            copy.wait()

    pl.run_scoped(run, pltpu.SemaphoreType.DMA((6,)))


def solution(mesh):
    in_specs = (
        P(None, "fsdp", "member"),
        P("fsdp", "member"),
        P("fsdp", "member"),
        P(None, "member"),
        P(None, "member"),
        P(None, "fsdp", "member"),
    )
    out_specs = (
        P(None, "fsdp", "member"),
        P(None, "fsdp", "member"),
        P("fsdp", "member"),
        P(None, "member"),
        P(None, "member"),
        P("fsdp", "member"),
    )
    members = mesh.shape["member"]
    chips = mesh.shape["fsdp"] // 2
    if members == 2 and chips >= 8 and chips & (chips - 1) == 0:
        per_device = functools.partial(fused, chips)
    else:
        per_device = general
    return jax.shard_map(
        per_device, mesh=mesh, in_specs=in_specs, out_specs=out_specs, check_vma=False
    )
```

```python
import functools

import jax
import jax.numpy as jnp
from jax import lax
from jax.experimental import pallas as pl
from jax.experimental.pallas import tpu as pltpu
from jax.sharding import PartitionSpec as P

F32 = jnp.float32
BF16 = jnp.bfloat16


def general(context, residual, out_weight, in_factor, out_factor, cotangent):
    in_wide = in_factor.astype(jnp.float32)
    out_wide = out_factor.astype(jnp.float32)
    scaled_local = (context.astype(jnp.float32) * in_wide[:, None, :]).astype(jnp.bfloat16)
    scaled_grad = (cotangent.astype(jnp.float32) * out_wide[:, None, :]).astype(jnp.bfloat16)
    scaled_context = lax.all_gather(scaled_local, "member", axis=2, tiled=True)
    weight = lax.all_gather(out_weight, "fsdp", axis=0, tiled=True)
    projected = jnp.einsum(
        "eti,id->etd", scaled_context, weight, preferred_element_type=jnp.float32
    )
    partial_value = jnp.einsum(
        "etd,id->eti", scaled_grad, weight, preferred_element_type=jnp.float32
    )
    hidden = (residual.astype(jnp.float32)[None] + projected * out_wide[:, None, :]).astype(
        jnp.bfloat16
    )
    backward = lax.psum_scatter(
        partial_value.astype(jnp.bfloat16), "member", scatter_dimension=2, tiled=True
    ).astype(jnp.float32)
    grad_context = (backward * in_wide[:, None, :]).astype(jnp.bfloat16)
    grad_in_local = jnp.sum(context.astype(jnp.float32) * backward, axis=1)
    grad_out_local = jnp.sum(cotangent.astype(jnp.float32) * projected, axis=1)
    grad_in, grad_out = lax.psum((grad_in_local, grad_out_local), "fsdp")
    grad_block = jnp.einsum(
        "eti,etd->id", scaled_context, scaled_grad, preferred_element_type=jnp.float32
    )
    grad_weight = lax.psum_scatter(grad_block, "fsdp", scatter_dimension=0, tiled=True)
    grad_residual = jnp.sum(cotangent.astype(jnp.float32), axis=0)
    return (hidden, grad_context, grad_weight, grad_in, grad_out, grad_residual)


def kernel(C, *refs):
    half = C // 2
    far = C // 2
    dma = pltpu.SemaphoreType.DMA
    pl.run_scoped(
        functools.partial(work, C, *refs),
        dma((6,)),
        dma((6,)),
        dma((13,)),
        dma((half + 1,)),
        dma((2 * far - 1,)),
        dma((far + 1,)),
        dma((half + 1,)),
        dma((C,)),
        dma((2 * far - 1,)),
        dma((7,)),
        pltpu.SemaphoreType.REGULAR,
    )


def work(
    C,
    ctx_h, res_h, w_h, inf_h, outf_h, cot_h,
    hid_o, gc_o, gw_o, gi_o, go_o, gr_o,
    hid, gc, gw, gi, go, gr,
    ctx, cot, res, inf, outf, cbuf, infx, sc, sg, wb, proj, part, xrecv, gall, psend, precv, rsend, rrecv,
    arb, ars, arr, fin, swp, swr, relay,
    ld_sem, st_sem, out_sem, cx_rs, ag_rs, pt_rs, px_rs, ps_rs, rs_rs, ar_rs, ready,
):
    E, T, H = ctx.shape
    R = w_h.shape[0]
    R2 = 2 * R
    S = R // 2
    half = C // 2
    far = C // 2
    lines = C // 2
    H2 = H // 2
    pieces = 2 * far - 1

    m = lax.axis_index("member")
    f = lax.axis_index("fsdp")
    c = f % 2
    q = f // 2
    p = (1 - q % 2) * (q // 2) + (q % 2) * (C - 1 - q // 2)

    def chip_at(offset):
        pos = (p + offset + C) % C
        y = pos // half
        return 2 * ((1 - y) * pos + y * (C - 1 - pos)) + y

    peer = (1 - m, f)
    partner = (m, q * 2 + 1 - c)
    nxt = (m, chip_at(1) * 2 + c)
    prv = (m, chip_at(-1) * 2 + c)
    side = (nxt, prv)
    sign = (1, -1)
    beside = (m, f + 2 - 4 * (q % 2))

    def along(i):
        line = q // 2
        other = 0
        bit = 1
        while bit < lines:
            own = (line // bit) % 2
            other = other + bit * (1 - own if i & bit else own)
            bit *= 2
        return (m, f + 4 * (other - line))


    def rc(src, dst, ss, rs, dev):
        return pltpu.make_async_remote_copy(
            src_ref=src, dst_ref=dst, send_sem=ss, recv_sem=rs,
            device_id=dev, device_id_type=pl.DeviceIdType.MESH,
        )

    barrier = pltpu.get_barrier_semaphore()

    def greet(dev):
        pl.semaphore_signal(barrier, inc=1, device_id=dev, device_id_type=pl.DeviceIdType.MESH)

    lead, deputy = m * c == 1, m * (1 - c) == 1
    greet((1 - m, q * 2 + c + (1 - m) * (1 - c)))

    @pl.when(jnp.logical_not(lead))
    def _():
        greet(partner)

    for ahead in (1, -1):
        greet((m, chip_at(ahead) * 2 + c * (1 - m)))

    def rows_of(core):
        return pl.ds(pl.multiple_of(core * R, R), R)

    def store(i, src, dst):
        pltpu.make_async_copy(src, dst, st_sem.at[i]).start()

    CX, CXF, CXP, AG, PT, PX, PS, RS, AR, SWAP, SWP, FIN, RELAY = range(13)

    def load(i, src, dst):
        return pltpu.make_async_copy(src, dst, ld_sem.at[i])

    ld_inf = load(0, inf_h, inf)
    ld_ctx = load(1, ctx_h, ctx)
    ld_outf = load(2, outf_h, outf)
    ld_cot = load(3, cot_h, cot)
    ld_w = load(4, w_h, wb.at[q, rows_of(c)])
    ld_res = load(5, res_h, res)

    def load_all():
        for copy in (ld_inf, ld_ctx, ld_outf, ld_cot, ld_w, ld_res):
            copy.start()

    pl.when(m == 0)(load_all)

    order = [chip_at(-far)] + [chip_at(s * (far - k)) for k in range(1, far) for s in sign] + [q]

    def ranked(side_of):
        found = [0] * half
        count = 0
        for chip in order:
            member = chip // half == side_of
            for n in range(half):
                found[n] = jnp.where(jnp.logical_and(member, count == n), chip, found[n])
            count = count + jnp.where(member, 1, 0)
        return found

    mine = ranked(m)
    theirs = ranked(1 - m)

    def cols_of(chip):
        return pl.ds(pl.multiple_of((chip % half) * R2, R2), R2)

    def cx(n):
        return rc(ctx_h.at[:, :, cols_of(mine[n])], cbuf.at[n], out_sem.at[CX], cx_rs.at[n], peer)

    cxf = rc(inf_h, infx, out_sem.at[CXF], cx_rs.at[half], peer)

    cxp = rc(infx, infx, out_sem.at[CXP], cx_rs.at[half], partner)

    def pass_on():
        cxf.wait_recv()
        cxp.start()

    def sub(core, u):
        return pl.ds(pl.multiple_of(core * R + u * S, S), S)

    def ag(d, s, u, shift):
        qq = chip_at(-sign[d] * (s - 1 + shift))
        dst = wb.at[qq, sub(c, u)]
        src = w_h.at[pl.ds(u * S, S)] if (s == 1 and shift == 0) else dst
        return rc(src, dst, out_sem.at[AG], ag_rs.at[2 * (s - 1) + int(u != d)], side[d])

    def pt(s, u, offset, own):
        qq = chip_at(offset)
        dst = wb.at[qq, sub(c if own else 1 - c, u)]
        src = w_h.at[pl.ds(u * S, S)] if (own and s == 0) else dst
        return rc(src, dst, out_sem.at[PT], pt_rs.at[s], partner)

    def both_wait(sems, i):
        held = wb.at[q, rows_of(c)]
        rc(held, held, out_sem.at[AG], sems.at[i], nxt).wait_recv()

    def pt_wait(s):
        held = wb.at[q] if 0 < s < far else wb.at[q, rows_of(c)]
        rc(held, held, out_sem.at[PT], pt_rs.at[s], partner).wait_recv()

    def tell(sem):
        pl.semaphore_signal(sem, inc=1, device_id=partner, device_id_type=pl.DeviceIdType.MESH)

    @pl.when(jnp.logical_not(deputy))
    def _():
        pl.semaphore_wait(barrier, 4 - m)

    @pl.when(lead)
    def _():
        tell(ready)

    @pl.when(deputy)
    def _():
        pl.semaphore_wait(ready, 1)

    pl.when(c == 1)(cxf.start)
    for n in range(half):
        cx(n).start()
    pl.when(m != 0)(load_all)

    @pl.when(deputy)
    def _():
        pl.semaphore_wait(barrier, 4)
        tell(ready)

    @pl.when(lead)
    def _():
        pl.semaphore_wait(ready, 1)

    for t in range(2):
        for d in range(2):
            ag(d, 1, d if t == 0 else 1 - d, 0).start()
        pt(0, t, 0, True).start()

    ld_inf.wait()
    ld_ctx.wait()
    inw = inf[...].astype(F32)
    for e in range(E):
        v = (ctx[e].astype(F32) * inw[e:e + 1]).astype(BF16)
        for j in range(half):
            sc[m * half + j, e * T:(e + 1) * T, :] = v[:, j * R2:(j + 1) * R2]
    ld_outf.wait()
    ld_cot.wait()
    outw = outf[...].astype(F32)
    for e in range(E):
        sg[e * T:(e + 1) * T, :] = (cot[e].astype(F32) * outw[e:e + 1]).astype(BF16)

    def px(qq, first, end, last=False):
        rows = pl.ds(first * T, (end - first) * T)
        i = half if last else qq % half
        return rc(part.at[qq, rows], xrecv.at[qq % half, rows], out_sem.at[PX], px_rs.at[i], peer)

    last_rows = pl.ds((E - 1) * T, T)
    relay_in = rc(part.at[theirs[0], last_rows], relay, out_sem.at[PX], ar_rs.at[6], partner)
    relay_out = rc(
        relay, xrecv.at[theirs[0] % half, last_rows], out_sem.at[RELAY], px_rs.at[half], (1 - m, q * 2)
    )

    def ps(qq):
        return rc(psend.at[qq], precv.at[qq], out_sem.at[PS], ps_rs.at[qq], partner)

    def gw_one(qq):
        g = lax.dot_general(sc[qq], sg[...], (((0,), (0,)), ((), ())), preferred_element_type=F32)
        gall[qq, 0] = g[:R]
        gall[qq, 1] = g[R:]
        psend[qq] = gall[qq, 1 - c].astype(BF16)
        ps(qq).start()

    def order_at(i):
        return chip_at((far - (i + 1) // 2) * (1 - 2 * ((i + 1) % 2)))

    def gw_mine():
        def body(i, carry):
            qq = order_at(i)

            @pl.when(qq // half == m)
            def _():
                gw_one(qq)
            return carry
        lax.fori_loop(0, C, body, 0)

    def project(qq):
        proj[...] += jnp.dot(sc[qq], wb[qq], preferred_element_type=F32)

    def process(offsets):
        def body(j, carry):
            off = offsets[0] if len(offsets) == 1 else offsets[0] + j * (offsets[1] - offsets[0])
            qq = chip_at(off)
            part[qq] = lax.dot_general(
                sg[...], wb[qq], (((1,), (1,)), ((), ())), preferred_element_type=F32
            ).astype(BF16)

            @pl.when(jnp.logical_and(qq // half != m, qq != theirs[0]))
            def _():
                px(qq, 0, E).start()

            @pl.when(jnp.logical_and(c == 1, qq == theirs[0]))
            def _():
                px(qq, 0, E - 1).start()

            @pl.when(jnp.logical_and(c == 0, qq == theirs[0]))
            def _():
                px(qq, 0, E - 2).start()
                relay_in.start()

            @pl.when(qq // half == m)
            def _():
                project(qq)
            return carry
        lax.fori_loop(0, len(offsets), body, 0)

    def piece(k, u, d):
        return 2 * k - 1 + int(u == d) if k else 0

    def rs(d, k, u):
        i = piece(k, u, d)
        return rc(rsend.at[d, i], rrecv.at[d, i], out_sem.at[RS], rs_rs.at[i], side[d])

    def chip_sum(qq, u):
        rows = slice(u * S, (u + 1) * S)
        return gall[qq, c, rows, :] + precv[qq, rows, :].astype(F32)

    def rs_sub(k, late):
        chips = [chip_at(sign[d] * (far - k)) if k else chip_at(-far) for d in range(2)]
        if k == 0:
            ps(chips[0]).wait_recv()
        elif not late:
            for d in range(2):
                ps(chips[d]).wait_recv()
        held = k > 1 or (k == 1 and late)
        if held:
            both_wait(rs_rs, piece(k - 1, int(late), 1))
        for d in range(2):
            u = d if late else 1 - d
            v = chip_sum(chips[d], u)
            if held:
                v = v + rrecv[d, piece(k - 1, u, d)].astype(F32)
            rsend[d, piece(k, u, d)] = v.astype(BF16)
            rs(d, k, u).start()

    proj[...] = jnp.zeros(proj.shape, F32)
    gw_mine()
    ld_w.wait()
    pt_wait(0)
    process([0])

    def scale_in(n):
        cx(n).wait_recv()
        for e in range(E):
            wide = infx[e:e + 1, cols_of(theirs[n])].astype(F32)
            sc[theirs[n], e * T:(e + 1) * T, :] = (cbuf[n, e].astype(F32) * wide).astype(BF16)
        gw_one(theirs[n])

    def forward(s, t):
        both_wait(ag_rs, 2 * (s - 1) + t)
        for d in range(2):
            u = d if t == 0 else 1 - d
            if s + 1 < far or (s + 1 == far and t == 0):
                ag(d, s + 1, u, 0).start()
            pt(s, u, -sign[d] * s, True).start()

    for s in range(1, far):
        forward(s, 0)
        if s == far - 1:
            rs_sub(0, True)
        if s == 1:
            gr[...] = jnp.sum(cot[...].astype(F32), axis=0)
            store(1, gr, gr_o)
        else:
            pt_wait(s - 1)
            process([1 - s])
        forward(s, 1)
        if s == 1:
            pl.when(c == 1)(pass_on)
        if s > 1:
            process([s - 1])
            if s == 2:
                pl.when(c == 0)(cxp.wait_recv)
            scale_in(s - 2)
    scale_in(far - 2)
    both_wait(ag_rs, 2 * (far - 1))
    for d in range(2):
        pt(far, d, far, True).start()
    pt_wait(far - 1)
    process([1 - far])
    rs_sub(1, False)
    process([far - 1])
    pt_wait(far)
    process([far])
    for n in range(far - 1):
        project(theirs[n])
    rs_sub(1, True)
    for n in range(far - 1, half):
        scale_in(n)
        project(theirs[n])

    ld_res.wait()
    resw = res[...].astype(F32)
    for e in range(E):
        pe = proj[e * T:(e + 1) * T, :]
        hid[e] = (resw + pe * outw[e:e + 1]).astype(BF16)
        a = jnp.sum(cot[e].astype(F32) * pe, axis=0, keepdims=True)
        for h in range(2):
            arb[h, 2 * E + e:2 * E + e + 1, :] = a[:, h * H2:(h + 1) * H2]
    store(0, hid, hid_o)
    for n in range(half):
        h, first = n * R2 // H2, n * R2 % H2
        slot = theirs[n] % half
        ahead = slot * R2 // H2
        far_cols = pl.ds(pl.multiple_of(slot * R2 - ahead * H2, R2), R2)
        for e in range(E):
            rows = slice(e * T, (e + 1) * T)
            a = ctx[e, :, n * R2:(n + 1) * R2].astype(F32) * part[m * half + n, rows, :].astype(F32)
            arb[h, e:e + 1, first:first + R2] = jnp.sum(a, axis=0, keepdims=True)
            a = cbuf[n, e].astype(F32) * part[theirs[n], rows, :].astype(F32)
            arb[ahead, E + e:E + e + 1, far_cols] = jnp.sum(a, axis=0, keepdims=True)

    def ar(i, src, dev):
        return rc(src, arr.at[i], out_sem.at[AR], ar_rs.at[min(i, 2)], dev)

    to_partner = ar(0, arb.at[1 - c], partner)
    to_beside = ar(1, ars.at[0], beside)
    to_lines = [ar(1 + i, ars.at[1], along(i)) for i in range(1, lines)]
    from_lines = rc(arr.at[2:], arr.at[2:], out_sem.at[AR], ar_rs.at[2], partner)
    to_other = rc(fin.at[0], fin.at[1], out_sem.at[FIN], ar_rs.at[3], partner)
    swap = rc(swp, swr.at[c], out_sem.at[SWAP], ar_rs.at[4], peer)
    swap_on = rc(swr.at[c], swr.at[c], out_sem.at[SWP], ar_rs.at[5], partner)

    own_half = pl.ds(pl.multiple_of(c * H2, H2), H2)
    other_half = pl.ds(pl.multiple_of((1 - c) * H2, H2), H2)

    def ar_step(i):
        if i == 0:
            to_partner.wait_recv()
            ars[0] = arb[c] + arr[0]
            to_beside.start()
        elif i == 1:
            to_beside.wait_recv()
            ars[1] = ars[0] + arr[1]
            for copy in to_lines:
                copy.start()
        else:
            from_lines.wait_recv()
            total = ars[1]
            for n in range(2, lines + 1):
                total = total + arr[n]
            swp[...] = total[E:2 * E]
            fin[0, :E] = total[:E]
            fin[0, E:] = total[2 * E:]
            swap.start()
            to_other.start()

    def finish(n, members, i):
        chip = mine[n]
        slot = chip % half
        held = xrecv.at[slot, pl.ds(members[0] * T, len(members) * T)]
        rc(held, held, out_sem.at[PX], px_rs.at[i], peer).wait_recv()
        for e in members:
            rows = slice(e * T, (e + 1) * T)
            be = part[chip, rows, :].astype(F32) + xrecv[slot, rows, :].astype(F32)
            wide = inf[e:e + 1, cols_of(chip)].astype(F32)
            gc[e, :, cols_of(chip)] = (be * wide).astype(BF16)
        rows = pl.ds(members[0], len(members))
        store(2, gc.at[rows, :, cols_of(chip)], gc_o.at[rows, :, cols_of(chip)])

    every = range(E)

    to_partner.start()
    pending = half
    for k in range(2, far):
        rs_sub(k, False)
        if k == 2:
            ar_step(0)
        rs_sub(k, True)
        if k == 2:
            ar_step(1)
        if pending > 2:
            pending -= 1
            finish(pending, every, mine[pending] % half)
    ar_step(2)

    @pl.when(c == 1)
    def _():
        relay_in.wait_recv()
        relay_out.start()
        px(theirs[0], E - 1, E, True).start()

    @pl.when(c == 0)
    def _():
        px(theirs[0], E - 2, E - 1).start()

    ps(q).wait_recv()
    for t in range(2):
        both_wait(rs_rs, piece(far - 1, t, 1))
    for u in range(2):
        rows = slice(u * S, (u + 1) * S)
        total = chip_sum(q, u)
        for d in range(2):
            total = total + rrecv[d, piece(far - 1, u, d)].astype(F32)
        gw[rows, :] = total
        store(3, gw.at[pl.ds(u * S, S)], gw_o.at[pl.ds(u * S, S)])
    to_other.wait_recv()
    go[:, own_half] = fin[0, E:]
    go[:, other_half] = fin[1, E:]
    store(4, go, go_o)
    while pending > 1:
        pending -= 1
        finish(pending, every, mine[pending] % half)
    swap.wait_recv()
    swap_on.start()
    finish(0, every[:E - 1], mine[0] % half)
    finish(0, every[E - 1:], half)
    swap_on.wait_recv()
    gi[:, own_half] = fin[0, :E] + swr[c]
    gi[:, other_half] = fin[1, :E] + swr[1 - c]
    store(5, gi, gi_o)

    sent = (
        (CX, cbuf), (AG, rsend), (PT, psend), (PX, xrecv),
        (PS, psend), (RS, rsend), (AR, arr), (SWAP, swp), (SWP, swp), (FIN, fin.at[0]),
    )
    for i, ref in sent:
        rc(ref, ref, out_sem.at[i], ar_rs.at[4], peer).wait_send()

    @pl.when(c == 1)
    def _():
        cxf.wait_send()
        cxp.wait_send()
        relay_out.wait_send()

    stored = ((hid, hid_o), (gr, gr_o), (gc, gc_o), (gw, gw_o), (go, go_o), (gi, gi_o))
    for i, (src, dst) in enumerate(stored):
        pltpu.make_async_copy(src, dst, st_sem.at[i]).wait()


def fused(C, context, residual, out_weight, in_factor, out_factor, cotangent):
    E, T, H = context.shape
    M = E * T
    R = out_weight.shape[0]
    half = C // 2
    far = half
    lines = C // 2
    pieces = 2 * far - 1
    hbm = pl.BlockSpec(memory_space=pl.ANY)
    shape = jax.ShapeDtypeStruct
    results = pl.pallas_call(
        functools.partial(kernel, C),
        out_shape=(
            pltpu.VMEM((E, T, H), BF16),
            pltpu.VMEM((E, T, H), BF16),
            pltpu.VMEM((R, H), F32),
            pltpu.VMEM((E, H), F32),
            pltpu.VMEM((E, H), F32),
            pltpu.VMEM((T, H), F32),
        ),
        in_specs=[hbm] * 6,
        out_specs=tuple([hbm] * 6),
        scratch_shapes=[
            pltpu.VMEM((E, T, H), BF16),
            pltpu.VMEM((E, T, H), BF16),
            pltpu.VMEM((R, H), F32),
            pltpu.VMEM((E, H), F32),
            pltpu.VMEM((E, H), F32),
            pltpu.VMEM((T, H), F32),
            pltpu.VMEM((E, T, H), BF16),
            pltpu.VMEM((E, T, H), BF16),
            pltpu.VMEM((T, H), BF16),
            pltpu.VMEM((E, H), BF16),
            pltpu.VMEM((E, H), BF16),
            pltpu.VMEM((half, E, T, 2 * R), BF16),
            pltpu.VMEM((E, H), BF16),
            pltpu.VMEM((C, M, 2 * R), BF16),
            pltpu.VMEM((M, H), BF16),
            pltpu.VMEM((C, 2 * R, H), BF16),
            pltpu.VMEM((M, H), F32),
            pltpu.VMEM((C, M, 2 * R), BF16),
            pltpu.VMEM((half, M, 2 * R), BF16),
            pltpu.VMEM((C, 2, R, H), F32),
            pltpu.VMEM((C, R, H), BF16),
            pltpu.VMEM((C, R, H), BF16),
            pltpu.VMEM((2, pieces, R // 2, H), BF16),
            pltpu.VMEM((2, pieces, R // 2, H), BF16),
            pltpu.VMEM((2, 3 * E, H // 2), F32),
            pltpu.VMEM((2, 3 * E, H // 2), F32),
            pltpu.VMEM((lines + 1, 3 * E, H // 2), F32),
            pltpu.VMEM((2, 2 * E, H // 2), F32),
            pltpu.VMEM((E, H // 2), F32),
            pltpu.VMEM((2, E, H // 2), F32),
            pltpu.VMEM((T, 2 * R), BF16),
        ],
        compiler_params=pltpu.CompilerParams(
            collective_id=0, has_side_effects=True, vmem_limit_bytes=62208 * 1024
        ),
    )(context, residual, out_weight, in_factor, out_factor, cotangent)
    return pl.pallas_call(
        deliver,
        out_shape=tuple(shape(r.shape, r.dtype) for r in results),
        in_specs=[hbm] * 6,
        out_specs=tuple([hbm] * 6),
        compiler_params=pltpu.CompilerParams(vmem_limit_bytes=1024 * 1024),
    )(*results)


def deliver(*refs):
    def run(sem):
        copies = [pltpu.make_async_copy(refs[i], refs[6 + i], sem.at[i]) for i in range(6)]
        for copy in copies:
            copy.start()
        for copy in copies:
            copy.wait()

    pl.run_scoped(run, pltpu.SemaphoreType.DMA((6,)))


def solution(mesh):
    in_specs = (
        P(None, "fsdp", "member"),
        P("fsdp", "member"),
        P("fsdp", "member"),
        P(None, "member"),
        P(None, "member"),
        P(None, "fsdp", "member"),
    )
    out_specs = (
        P(None, "fsdp", "member"),
        P(None, "fsdp", "member"),
        P("fsdp", "member"),
        P(None, "member"),
        P(None, "member"),
        P("fsdp", "member"),
    )
    members = mesh.shape["member"]
    chips = mesh.shape["fsdp"] // 2
    if members == 2 and chips >= 8 and chips & (chips - 1) == 0:
        per_device = functools.partial(fused, chips)
    else:
        per_device = general
    return jax.shard_map(
        per_device, mesh=mesh, in_specs=in_specs, out_specs=out_specs, check_vma=False
    )
```
